32 devices in a mesh: prow: 8 (over y, x, core), pcol: 4 (over z).
Axes of the slice: x: 2, y: 2, z: 4, core: 2. Of those that a mesh axis runs over, the one named last changes fastest.
Arguments:
- inverse: bfloat16 [4, 4096, 8, 2048], P(None, 'prow', None, 'pcol'), may hold values from -6 to 6
- panel: bfloat16 [2, 4, 4096, 256], P(None, None, 'prow'), may hold values from -0.09375 to 0.09375
- structure: int32 [2, 8], replicated, may hold values from 0 to 31, as said below
- diag_inverse: float32 [2, 256, 256], replicated, may hold values from -6 to 6
Outputs:
- off_diag: bfloat16 [2, 4, 4096, 256], P(None, None, ('prow', 'pcol'))
- diag_block: float32 [2, 256, 256], replicated
The draws below stay inside these ranges and needn't reach their ends.
Inputs may be any that keep to these rules, and one draw needn't show every extreme that they name: `structure`: each row lists 8 distinct block indices in increasing order, exactly one of them congruent to p modulo 8 for every p, and always includes the last ancestor block 31.
All inputs are finite; a program needn't handle non-finite values.
Results may differ from the reference program's by a relative error of at most 0.0022.
Values may be sent and summed in bfloat16 or wider, within the bound.
A program may use at most 128 MiB of HBM per device.

```python
import jax
import jax.numpy as jnp

BLK = 512
W = 256
NODES = 2
BR_DEV = 4
BC_DEV = 8
SEL = 8
N_PROW = 8
N_PCOL = 4


def draw_structure(key, part):
    listed = []
    for supernode in range(NODES):
        subkey = jax.random.fold_in(key, 17 + supernode)
        offsets = jax.random.randint(subkey, (SEL,), 0, BR_DEV).astype(jnp.int32)
        offsets = offsets.at[SEL - 1].set(BR_DEV - 1)
        indices = offsets * SEL + jnp.arange(SEL, dtype=jnp.int32)
        listed.append(jnp.sort(indices))
    return jnp.stack(listed).astype(jnp.int32)


def block_levels(rng, extent, cuts, smallest, largest):
    level = 1.0
    for position, shards_of in cuts:
        heights = jax.random.uniform(jax.random.fold_in(jax.random.fold_in(rng, 6), position), (shards_of,), jnp.float32, smallest / len(cuts), largest / len(cuts))
        level = level * jnp.repeat(jnp.exp(heights), extent[position] // shards_of).reshape((-1,) + (1,) * (len(extent) - 1 - position))
    return level


def bell_draw(stream_key, extent, spread, bound, cuts=(), kind=jnp.bfloat16):
    array = spread * jax.random.normal(stream_key, extent, jnp.float32)
    if cuts:
        array = array * block_levels(stream_key, extent, cuts, -0.22, 0.18)
    return jnp.clip(array, -bound, bound).astype(kind)


def setup_inputs(seed: int = 0) -> dict:
    key_of = jax.random.split(jax.random.key(seed), 5)
    inverse = bell_draw(key_of[0], (BR_DEV, N_PROW * BLK, BC_DEV, N_PCOL * BLK), 1.0, 6.0, ((1, 8), (3, 4)))
    panel = bell_draw(key_of[1], (NODES, BR_DEV, N_PROW * BLK, W), (SEL * BLK) ** -0.5, 0.09375, ((2, 8),))
    structure = draw_structure(jax.random.fold_in(key_of[4], 71), 0)
    diag_inverse = bell_draw(key_of[3], (NODES, W, W), 1.0, 6.0, (), jnp.float32)
    return {"inverse": inverse, "panel": panel, "structure": structure, "diag_inverse": diag_inverse}


def reference(inverse, panel, structure, diag_inverse):
    total_blocks = BR_DEV * N_PROW
    blocks = inverse.reshape(total_blocks, BLK, total_blocks, BLK)
    pieces = []
    products = []
    for supernode in range(NODES):
        chosen = structure[supernode]
        factor_blocks = panel[supernode].reshape(total_blocks, BLK, W)
        factor_rows = jnp.take(factor_blocks, chosen, axis=0).reshape(SEL * BLK, W)
        picked = jnp.take(jnp.take(blocks, chosen, axis=0), chosen, axis=2).reshape(SEL * BLK, SEL * BLK)
        result = (-jnp.dot(picked, factor_rows, preferred_element_type=jnp.float32)).astype(jnp.bfloat16)
        placed = jnp.zeros((total_blocks, BLK, W), jnp.bfloat16).at[chosen].set(result.reshape(SEL, BLK, W))
        pieces.append(placed.reshape(BR_DEV, N_PROW * BLK, W))
        products.append(jnp.dot(factor_rows.T, result, preferred_element_type=jnp.float32))
    return jnp.stack(pieces), diag_inverse - jnp.stack(products)
```

```python
import functools

import jax
import jax.numpy as jnp
from jax import lax
from jax.experimental import pallas as pl
from jax.experimental.pallas import tpu as pltpu
from jax.sharding import PartitionSpec as P

MESH = pl.DeviceIdType.MESH
SUB = 2
STRIPS = 8
FULL = 32700.0


def remote(src, dst, send, recv, p, q):
    return pltpu.make_async_remote_copy(
        src_ref=src, dst_ref=dst, send_sem=send, recv_sem=recv, device_id=(p, q), device_id_type=MESH
    )


def scope(name):
    return jax.named_scope(name)


def selected(
    n_rows, n_cols, structure_hbm, inverse_ref, panel_ref, d_ref, y_ref, g_ref,
    structure_ref, panel_buf, raw, wide, a_ref, l_ref, l_buf, part,
    right_buf, left_buf, right_scale, left_scale,
    term, term_buf, term_scale, plane_buf, plane_scale, col_buf, col_scale, gath, gath_scale,
    s_sem, n_sem, a_sem,
    l_send, l_recv, r_send, r_recv, f_send, f_recv, p_send, p_recv, c_send, c_recv, g_send, g_recv,
):
    p = lax.axis_index("prow")
    q = lax.axis_index("pcol")
    nodes, ratio, block, width = l_buf.shape
    rows_local, _, cols_local, _ = inverse_ref.shape
    listed = structure_ref.shape[1]
    piece = block // n_cols
    seg = width // n_rows
    chunk = block // (2 * SUB)
    strip = block // STRIPS
    hi = p // n_cols
    lo = p % n_cols
    t = jnp.int32(0)
    bit = 1
    while bit < n_cols:
        t = t + bit * (((lo // bit) + (q // bit)) % 2)
        bit *= 2
    pair = p + 1 - 2 * (p % 2)

    def beside(j):
        lo2 = jnp.int32(0)
        b = 1
        while b < n_cols:
            lo2 = lo2 + b * (((lo // b) + (2 * j // b)) % 2)
            b *= 2
        return hi * n_cols + lo2

    structure_copy = pltpu.make_async_copy(structure_hbm, structure_ref, s_sem)
    structure_copy.start()
    panel_copies = [pltpu.make_async_copy(panel_ref.at[s], panel_buf[s], n_sem.at[s]) for s in range(nodes)]
    for copy in panel_copies:
        copy.start()

    def strip_copy(k):
        part_of = pl.ds(k * strip, strip)
        return pltpu.make_async_copy(inverse_ref.at[:, part_of], raw[k], a_sem.at[k])

    for k in range(STRIPS):
        strip_copy(k).start()

    barrier = pltpu.get_barrier_semaphore()
    for k in range(1, n_rows):
        pl.semaphore_signal(barrier, inc=1, device_id=((p + k) % n_rows, q), device_id_type=MESH)
    for k in range(1, n_cols):
        pl.semaphore_signal(barrier, inc=1, device_id=(p, (q + k) % n_cols), device_id_type=MESH)

    def find(s, residue, divisor):
        found = jnp.int32(0)
        for i in range(listed):
            value = structure_ref[s, i]
            found = found + jnp.where(value % n_rows == residue, value // divisor, 0)
        return found

    with scope("pickl"):
        structure_copy.wait()
        row = [find(s, p, n_rows) for s in range(nodes)]
        cols = [[find(s, h * n_cols + q, n_cols) for h in range(ratio)] for s in range(nodes)]
        for s in range(nodes):
            panel_copies[s].wait()
            l_ref[s] = panel_buf[s][row[s]]

    with scope("barrier"):
        pl.semaphore_wait(barrier, n_rows + n_cols - 2)

    def rows(c):
        return pl.ds(pl.multiple_of(c * chunk, chunk), chunk)

    def l_slot(s, h, c):
        return l_buf.at[s, h, rows(c)]

    def to_peer_hi(s, c, k, src):
        return remote(src, l_slot(s, hi, c), l_send.at[s, c, k - 1], l_recv.at[s, hi, c],
                      (p + k * n_cols) % n_rows, q)

    def to_x(s, c, j, src):
        return remote(src, l_slot(s, hi, c), l_send.at[s, c, ratio - 1 + j - 1], l_recv.at[s, hi, c],
                      beside(j), q)

    def to_pair(s, c, k, src):
        h = (hi + k) % ratio
        return remote(src, l_slot(s, h, c), l_send.at[s, c, ratio - 1 + n_cols // 2 - 1 + k],
                      l_recv.at[s, h, c], pair, q)

    def l_arrived(s, c, h):
        remote(l_slot(s, h, c), l_slot(s, h, c), l_send.at[s, c, 0], l_recv.at[s, h, c], pair, q).wait_recv()

    owner = t == 0
    source_chip = t < 2
    core = p % 2

    def mine(u):
        return core * SUB + u

    def other(u):
        return (1 - core) * SUB + u

    @pl.when(owner)
    def _():
        for s in range(nodes):
            for u in range(SUB):
                to_pair(s, other(u), 0, l_ref.at[s, rows(other(u))]).start()
            for u in range(SUB):
                src = l_ref.at[s, rows(mine(u))]
                for j in range(1, n_cols // 2):
                    to_x(s, mine(u), j, src).start()
                for k in range(1, ratio):
                    to_peer_hi(s, mine(u), k, src).start()
            for u in range(SUB):
                to_pair(s, mine(u), 0, l_ref.at[s, rows(mine(u))]).start()
        for s in range(nodes):
            l_buf[s, hi] = l_ref[s]

    def own_from_pair(s, u):
        c = mine(u)

        @pl.when(t == 1)
        def _():
            l_arrived(s, c, hi)
            for j in range(1, n_cols // 2):
                to_x(s, c, j, l_slot(s, hi, c)).start()
            for k in range(1, ratio):
                to_peer_hi(s, c, k, l_slot(s, hi, c)).start()

    def own_from_x(s, u):
        c = mine(u)

        @pl.when(jnp.logical_not(source_chip))
        def _():
            l_arrived(s, c, hi)
            for k in range(1, ratio):
                to_peer_hi(s, c, k, l_slot(s, hi, c)).start()
            to_pair(s, c, 0, l_slot(s, hi, c)).start()

    def others_from_hi(s, u):
        c = mine(u)
        for k in range(1, ratio):
            l_arrived(s, c, (hi + k) % ratio)
            to_pair(s, c, k, l_slot(s, (hi + k) % ratio, c)).start()

    def rest(s):
        for u in range(SUB):
            c = other(u)

            @pl.when(jnp.logical_not(owner))
            def _():
                l_arrived(s, c, hi)

            for k in range(1, ratio):
                l_arrived(s, c, (hi + k) % ratio)

    def drain_blocks(s):
        for u in range(SUB):
            c = mine(u)
            src = l_slot(s, hi, c)
            for k in range(1, ratio):
                to_peer_hi(s, c, k, src).wait_send()
                to_pair(s, c, k, src).wait_send()

            @pl.when(source_chip)
            def _():
                for j in range(1, n_cols // 2):
                    to_x(s, c, j, src).wait_send()

            @pl.when(t != 1)
            def _():
                to_pair(s, c, 0, src).wait_send()

            @pl.when(owner)
            def _():
                to_pair(s, other(u), 0, src).wait_send()

    def choose(k):
        strip_copy(k).wait()
        for s in range(nodes):
            for b in range(block // 128):
                lanes = raw[k][row[s], :, :, b * 128:(b + 1) * 128].astype(jnp.float32)
                wide[s, b] = lanes.reshape(strip * cols_local, 128)
            for h in range(ratio):
                for b in range(block // 128):
                    a_ref[s, h, k * strip:(k + 1) * strip, b * 128:(b + 1) * 128] = wide[
                        s, b, pl.ds(cols[s][h], strip, stride=cols_local)
                    ].astype(jnp.bfloat16)

    def multiply(s):
        total = jnp.dot(a_ref[s, 0], l_buf[s, 0], preferred_element_type=jnp.float32)
        for h in range(1, ratio):
            total += jnp.dot(a_ref[s, h], l_buf[s, h], preferred_element_type=jnp.float32)
        for d in range(n_cols):
            part[s, d] = total[d * piece:(d + 1) * piece]
        return total

    def encoded(value):
        largest = jnp.maximum(jnp.max(jnp.abs(value), axis=0, keepdims=True), 1e-30)
        whole = jnp.floor(value * (FULL / largest) + 0.5).astype(jnp.int32).astype(jnp.int16)
        return whole, largest * (1.0 / FULL)

    def decoded(whole, scale):
        return whole.astype(jnp.int32).astype(jnp.float32) * scale

    def diagonal_term(s, total):
        high = total.astype(jnp.bfloat16)
        low = (total - high.astype(jnp.float32)).astype(jnp.bfloat16)
        over_rows = (((0,), (0,)), ((), ()))
        product = lax.dot_general(l_ref[s], high, over_rows, preferred_element_type=jnp.float32)
        product += lax.dot_general(l_ref[s], low, over_rows, preferred_element_type=jnp.float32)
        whole, scale = encoded(product)
        term_scale[s] = scale
        for k in range(n_rows):
            term[s, k] = product[k * seg:(k + 1) * seg]
            term_buf[s, k] = whole[k * seg:(k + 1) * seg]

    class both:
        def __init__(self, src, src_scale, dst, dst_scale, send, recv, send_at, recv_at, to_p, to_q):
            self.copies = [
                remote(src, dst, send.at[(0, *send_at)], recv.at[(0, *recv_at)], to_p, to_q),
                remote(src_scale, dst_scale, send.at[(1, *send_at)], recv.at[(1, *recv_at)], to_p, to_q),
            ]

        def start(self):
            for copy in self.copies:
                copy.start()

        def wait_send(self):
            for copy in self.copies:
                copy.wait_send()

        def wait_recv(self):
            for copy in self.copies:
                copy.wait_recv()

    def right_copy(s, d):
        return both(right_buf.at[s, d], right_scale.at[s, d], right_buf.at[s, d], right_scale.at[s, d],
                    r_send, r_recv, (s, d), (s, d), p, (q + 1) % n_cols)

    def left_copy(s, d):
        return both(left_buf.at[s, d], left_scale.at[s, d], left_buf.at[s, d], left_scale.at[s, d],
                    f_send, f_recv, (s, d), (s, d), p, (q + n_cols - 1) % n_cols)

    def right_send(s, d, value):
        right_buf[s, d], right_scale[s, d] = encoded(value)
        right_copy(s, d).start()

    def left_send(s, d, value):
        left_buf[s, d], left_scale[s, d] = encoded(value)
        left_copy(s, d).start()

    def line_start(s, nearest):
        @pl.when(q == 0)
        def _():
            for d in ((1,) if nearest else range(n_cols - 1, 1, -1)):
                right_send(s, d, part[s, d])

        @pl.when(q == n_cols - 1)
        def _():
            for d in ((n_cols - 2,) if nearest else range(n_cols - 2)):
                left_send(s, d, part[s, d])

    def relay_right(s):
        for d in range(n_cols - 1, 1, -1):
            @pl.when(jnp.logical_and(q > 0, q < d))
            def _():
                right_copy(s, d).wait_recv()
                right_send(s, d, decoded(right_buf[s, d], right_scale[s, d]) + part[s, d])

    def relay_left(s):
        for e in range(n_cols - 2):
            @pl.when(jnp.logical_and(q < n_cols - 1, q > e))
            def _():
                left_copy(s, e).wait_recv()
                left_send(s, e, decoded(left_buf[s, e], left_scale[s, e]) + part[s, e])

    left_half = 2 * q < n_cols - 1

    def relay(s, first):
        @pl.when(left_half)
        def _():
            (relay_right if first else relay_left)(s)

        @pl.when(jnp.logical_not(left_half))
        def _():
            (relay_left if first else relay_right)(s)

    def line_finish(s):
        @pl.when(q > 0)
        def _():
            right_copy(s, q).wait_recv()
            part[s, q] = part[s, q] + decoded(right_buf[s, q], right_scale[s, q])

        @pl.when(q < n_cols - 1)
        def _():
            left_copy(s, q).wait_recv()
            part[s, q] = part[s, q] + decoded(left_buf[s, q], left_scale[s, q])

        value = (-part[s, q]).astype(jnp.bfloat16)
        for r in range(rows_local):
            y_ref[s, r] = jnp.where(row[s] == r, value, jnp.zeros_like(value))

    def line_drain(s):
        for d in range(n_cols):
            @pl.when(q < d)
            def _():
                right_copy(s, d).wait_send()

            @pl.when(q > d)
            def _():
                left_copy(s, d).wait_send()

    def plane_copy(s, k):
        to = (p + k) % n_rows
        return both(term_buf.at[s, to], term_scale.at[s], plane_buf.at[s, n_rows - k], plane_scale.at[s, n_rows - k],
                    p_send, p_recv, (s, k), (s, n_rows - k), to, q)

    def plane_wait(s, k):
        both(term_buf.at[s, 0], term_scale.at[s], plane_buf.at[s, k], plane_scale.at[s, k],
             p_send, p_recv, (s, k), (s, k), pair, q).wait_recv()

    def col_copy(s, k):
        to = (q + k) % n_cols
        return both(col_buf.at[s, q], col_scale.at[s, q], col_buf.at[s, q], col_scale.at[s, q],
                    c_send, c_recv, (s, k), (s, n_cols - k), p, to)

    def col_wait(s, k):
        src = (q + k) % n_cols
        both(col_buf.at[s, src], col_scale.at[s, src], col_buf.at[s, src], col_scale.at[s, src],
             c_send, c_recv, (s, k), (s, k), pair, q).wait_recv()

    def gath_copy(s, k):
        to = (p + k) % n_rows
        return both(gath.at[s, p], gath_scale.at[s, p], gath.at[s, p], gath_scale.at[s, p],
                    g_send, g_recv, (s, k), (s, n_rows - k), to, q)

    def gath_wait(s, k):
        src = (p + k) % n_rows
        both(gath.at[s, src], gath_scale.at[s, src], gath.at[s, src], gath_scale.at[s, src],
             g_send, g_recv, (s, k), (s, k), pair, q).wait_recv()

    def plane_start(s):
        for k in range(1, n_rows):
            plane_copy(s, k).start()

    def col_start(s):
        total = term[s, p]
        for k in range(1, n_rows):
            plane_wait(s, k)
            total = total + decoded(plane_buf[s, k], plane_scale[s, k])
        col_buf[s, q], col_scale[s, q] = encoded(total)
        for k in range(1, n_cols):
            col_copy(s, k).start()

    def gath_start(s):
        for k in range(1, n_cols):
            col_wait(s, k)
        total = decoded(col_buf[s, 0], col_scale[s, 0])
        for k in range(1, n_cols):
            total = total + decoded(col_buf[s, k], col_scale[s, k])
        gath[s, p], gath_scale[s, p] = encoded(total)
        for k in range(1, n_rows):
            gath_copy(s, k).start()

    def finish_diagonal(s):
        for k in range(1, n_rows):
            gath_wait(s, k)
        for k in range(n_rows):
            part_of = slice(k * seg, (k + 1) * seg)
            g_ref[s, part_of] = d_ref[s, part_of] + decoded(gath[s, k], gath_scale[s, k])

    def after(s, total):
        with scope(f"line{s}"):
            line_start(s, False)
        with scope(f"diag{s}"):
            diagonal_term(s, total)
            plane_start(s)

    with scope("frompair"):
        for s in range(nodes):
            for u in range(SUB):
                own_from_pair(s, u)
    steps = []
    for s in range(nodes - 1):
        for u in range(SUB):
            steps.append((own_from_x, s, u))
        for u in range(SUB):
            steps.append((others_from_hi, s, u))
    k = 0
    for step, s, u in steps:
        with scope(f"choose{k}"):
            while k < STRIPS * (steps.index((step, s, u)) + 1) // (len(steps) + 1):
                choose(k)
                k += 1
        with scope(f"{step.__name__}{s}{u}"):
            step(s, u)
    with scope("chooserest"):
        for k in range(k, STRIPS):
            choose(k)
    for s in range(nodes - 1):
        with scope(f"own{s + 1}a"):
            own_from_x(s + 1, 0)
        with scope(f"rest{s}"):
            rest(s)
        with scope(f"mult{s}"):
            total = multiply(s)
        with scope(f"own{s + 1}b"):
            for u in range(1, SUB):
                own_from_x(s + 1, u)
        after(s, total)
    last = nodes - 1
    with scope("others1"):
        for u in range(SUB):
            others_from_hi(last, u)
    with scope("rest1"):
        rest(last)
    with scope("mult1"):
        total = multiply(last)
    after(last, total)
    for s in range(nodes):
        with scope(f"relayA{s}"):
            relay(s, True)
        with scope(f"colstart{s}"):
            col_start(s)
            line_start(s, True)
        with scope(f"relayB{s}"):
            relay(s, False)
    for s in range(nodes):
        with scope(f"gathstart{s}"):
            gath_start(s)
    for s in range(nodes):
        with scope(f"finish{s}"):
            line_finish(s)
    with scope("drain"):
        for s in range(nodes):
            drain_blocks(s)
            line_drain(s)
            for k in range(1, n_rows):
                plane_copy(s, k).wait_send()
            for k in range(1, n_cols):
                col_copy(s, k).wait_send()
    for s in range(nodes):
        with scope(f"findiag{s}"):
            finish_diagonal(s)
    for s in range(nodes):
        for k in range(1, n_rows):
            gath_copy(s, k).wait_send()


def on_device(inverse, panel, structure, diag_inverse):
    n_rows = lax.axis_size("prow")
    n_cols = lax.axis_size("pcol")
    rows_local, block, cols_local, _ = inverse.shape
    nodes, _, _, width = panel.shape
    ratio = n_rows // n_cols
    piece = block // n_cols
    seg = width // n_rows
    strip = block // STRIPS

    vmem = pl.BlockSpec(memory_space=pltpu.VMEM)
    hbm = pl.BlockSpec(memory_space=pltpu.HBM)
    f32, bf16, i16 = jnp.float32, jnp.bfloat16, jnp.int16
    dma = pltpu.SemaphoreType.DMA
    sends = ratio - 1 + n_cols // 2 - 1 + ratio
    return pl.pallas_call(
        functools.partial(selected, n_rows, n_cols),
        out_shape=(
            jax.ShapeDtypeStruct((nodes, rows_local, piece, width), bf16),
            jax.ShapeDtypeStruct((nodes, width, width), f32),
        ),
        in_specs=[hbm, hbm, hbm, vmem],
        out_specs=(vmem, vmem),
        scratch_shapes=[
            pltpu.SMEM(structure.shape, jnp.int32),
            tuple(pltpu.VMEM(panel.shape[1:], bf16) for _ in range(nodes)),
            tuple(pltpu.VMEM((rows_local, strip, *inverse.shape[2:]), bf16) for _ in range(STRIPS)),
            pltpu.VMEM((nodes, block // 128, strip * cols_local, 128), f32),
            pltpu.VMEM((nodes, ratio, block, block), bf16),
            pltpu.VMEM((nodes, block, width), bf16),
            pltpu.VMEM((nodes, ratio, block, width), bf16),
            pltpu.VMEM((nodes, n_cols, piece, width), f32),
            pltpu.VMEM((nodes, n_cols, piece, width), i16),
            pltpu.VMEM((nodes, n_cols, piece, width), i16),
            pltpu.VMEM((nodes, n_cols, 1, width), f32),
            pltpu.VMEM((nodes, n_cols, 1, width), f32),
            pltpu.VMEM((nodes, n_rows, seg, width), f32),
            pltpu.VMEM((nodes, n_rows, seg, width), i16),
            pltpu.VMEM((nodes, 1, width), f32),
            pltpu.VMEM((nodes, n_rows, seg, width), i16),
            pltpu.VMEM((nodes, n_rows, 1, width), f32),
            pltpu.VMEM((nodes, n_cols, seg, width), i16),
            pltpu.VMEM((nodes, n_cols, 1, width), f32),
            pltpu.VMEM((nodes, n_rows, seg, width), i16),
            pltpu.VMEM((nodes, n_rows, 1, width), f32),
            dma, dma((nodes,)), dma((STRIPS,)),
            dma((nodes, 2 * SUB, sends)), dma((nodes, ratio, 2 * SUB)),
            dma((2, nodes, n_cols)), dma((2, nodes, n_cols)),
            dma((2, nodes, n_cols)), dma((2, nodes, n_cols)),
            dma((2, nodes, n_rows)), dma((2, nodes, n_rows)),
            dma((2, nodes, n_cols)), dma((2, nodes, n_cols)),
            dma((2, nodes, n_rows)), dma((2, nodes, n_rows)),
        ],
        compiler_params=pltpu.CompilerParams(
            collective_id=0, has_side_effects=True, vmem_limit_bytes=50 * 1024 * 1024
        ),
        name="selected_inverse",
    )(structure, inverse, panel, diag_inverse)


def solution(mesh):
    placed = (P(None, "prow", None, "pcol"), P(None, None, "prow", None), P(), P())
    return jax.shard_map(
        on_device,
        mesh=mesh,
        in_specs=placed,
        out_specs=(P(None, None, ("prow", "pcol"), None), P()),
        check_vma=False,
    )
```

```python
import functools

import jax
import jax.numpy as jnp
from jax import lax
from jax.experimental import pallas as pl
from jax.experimental.pallas import tpu as pltpu
from jax.sharding import PartitionSpec as P

MESH = pl.DeviceIdType.MESH
SUB = 4
STRIPS = 8
AHEAD = 4
FULL = 32700.0


def remote(src, dst, send, recv, p, q):
    return pltpu.make_async_remote_copy(
        src_ref=src, dst_ref=dst, send_sem=send, recv_sem=recv, device_id=(p, q), device_id_type=MESH
    )


def scope(name):
    return jax.named_scope(name)


def find_row(structure_ref, s, residue, n_rows, divisor):
    found = jnp.int32(0)
    for i in range(structure_ref.shape[1]):
        value = structure_ref[s, i]
        found = found + jnp.where(value % n_rows == residue, value // divisor, 0)
    return found


def selected(
    n_rows, n_cols, structure_hbm, inverse_ref, panel_ref, y_out, g_out, scale_out,
    structure_ref, y_ref, own, own_scale, panel_buf, raw, wide, a_ref, l_ref, l_buf, part,
    right_buf, left_buf, right_scale, left_scale,
    term, term_buf, term_scale, plane_buf, plane_scale, col_own, col_own_scale, col_buf, col_scale,
    s_sem, n_sem, a_sem, o_sem,
    l_send, l_recv, r_send, f_send, r_recv, p_send, p_recv, c_send, c_recv, g_send, g_recv,
):
    p = lax.axis_index("prow")
    q = lax.axis_index("pcol")
    nodes, ratio, block, width = l_buf.shape
    rows_local, _, cols_local, _ = inverse_ref.shape
    piece = block // n_cols
    seg = width // n_rows
    chunk = block // (2 * SUB)
    strip = block // STRIPS
    hi = p // n_cols
    lo = p % n_cols
    t = jnp.int32(0)
    bit = 1
    while bit < n_cols:
        t = t + bit * (((lo // bit) + (q // bit)) % 2)
        bit *= 2
    pair = p + 1 - 2 * (p % 2)

    def beside(j):
        lo2 = jnp.int32(0)
        b = 1
        while b < n_cols:
            lo2 = lo2 + b * (((lo // b) + (2 * j // b)) % 2)
            b *= 2
        return hi * n_cols + lo2

    structure_copy = pltpu.make_async_copy(structure_hbm, structure_ref, s_sem)
    structure_copy.start()
    panel_copies = [pltpu.make_async_copy(panel_ref.at[s], panel_buf[s], n_sem.at[s]) for s in range(nodes)]
    for copy in panel_copies:
        copy.start()

    def strip_copy(k):
        part_of = pl.ds(k * strip, strip)
        return pltpu.make_async_copy(inverse_ref.at[:, part_of], raw[k], a_sem.at[k % AHEAD])

    barrier = pltpu.get_barrier_semaphore()
    for k in range(1, n_rows):
        pl.semaphore_signal(barrier, inc=1, device_id=((p + k) % n_rows, q), device_id_type=MESH)
    for k in range(1, n_cols):
        pl.semaphore_signal(barrier, inc=1, device_id=(p, (q + k) % n_cols), device_id_type=MESH)

    def find(s, residue, divisor):
        return find_row(structure_ref, s, residue, n_rows, divisor)

    with scope("pickl"):
        structure_copy.wait()
        row = [find(s, p, n_rows) for s in range(nodes)]
        cols = [[find(s, h * n_cols + q, n_cols) for h in range(ratio)] for s in range(nodes)]
        for s in range(nodes):
            panel_copies[s].wait()
            l_ref[s] = panel_buf[s][row[s]]
        for k in range(AHEAD):
            strip_copy(k).start()

    with scope("barrier"):
        pl.semaphore_wait(barrier, n_rows + n_cols - 2)

    def rows(c):
        return pl.ds(pl.multiple_of(c * chunk, chunk), chunk)

    def l_slot(s, h, c):
        return l_buf.at[s, h, rows(c)]

    def to_peer_hi(s, c, k, src):
        return remote(src, l_slot(s, hi, c), l_send.at[s, k - 1], l_recv.at[s, hi, c % SUB],
                      (p + k * n_cols) % n_rows, q)

    def to_x(s, c, j, src):
        return remote(src, l_slot(s, hi, c), l_send.at[s, ratio - 1 + j - 1], l_recv.at[s, hi, c % SUB],
                      beside(j), q)

    def to_pair(s, c, k, src):
        h = (hi + k) % ratio
        return remote(src, l_slot(s, h, c), l_send.at[s, ratio - 1 + n_cols // 2 - 1 + k],
                      l_recv.at[s, h, SUB], pair, q)

    def hand_over(s, c):
        return remote(l_ref.at[s, rows(c)], l_slot(s, hi, c), l_send.at[s, 2 * ratio - 1 + n_cols // 2 - 1],
                      l_recv.at[s, hi, c % SUB], pair, q)

    def l_arrived(s, c, h):
        remote(l_slot(s, h, c), l_slot(s, h, c), l_send.at[s, 0], l_recv.at[s, h, c % SUB], pair, q).wait_recv()

    def half(s, h):
        return l_buf.at[s, h, pl.ds(0, SUB * chunk)]

    def half_arrived(s, h):
        remote(half(s, h), half(s, h), l_send.at[s, 0], l_recv.at[s, h, SUB], pair, q).wait_recv()

    def half_sent(s, i):
        remote(half(s, 0), half(s, 0), l_send.at[s, i], l_recv.at[s, 0, 0], pair, q).wait_send()

    owner = t == 0
    source_chip = t < 2
    core = p % 2

    def mine(u):
        return core * SUB + u

    def other(u):
        return (1 - core) * SUB + u

    @pl.when(owner)
    def _():
        for s in range(nodes):
            for u in range(SUB):
                hand_over(s, other(u)).start()
            for u in range(SUB):
                src = l_ref.at[s, rows(mine(u))]
                for j in range(1, n_cols // 2):
                    to_x(s, mine(u), j, src).start()
                for k in range(1, ratio):
                    to_peer_hi(s, mine(u), k, src).start()
            for u in range(SUB):
                to_pair(s, mine(u), 0, l_ref.at[s, rows(mine(u))]).start()
        for s in range(nodes):
            l_buf[s, hi] = l_ref[s]

    def own_from_pair(s, u):
        c = mine(u)

        @pl.when(t == 1)
        def _():
            l_arrived(s, c, hi)
            for j in range(1, n_cols // 2):
                to_x(s, c, j, l_slot(s, hi, c)).start()
            for k in range(1, ratio):
                to_peer_hi(s, c, k, l_slot(s, hi, c)).start()

    def own_from_x(s, u):
        c = mine(u)

        @pl.when(jnp.logical_not(source_chip))
        def _():
            l_arrived(s, c, hi)
            for k in range(1, ratio):
                to_peer_hi(s, c, k, l_slot(s, hi, c)).start()
            to_pair(s, c, 0, l_slot(s, hi, c)).start()

    def others_from_hi(s, u):
        c = mine(u)
        for k in range(1, ratio):
            l_arrived(s, c, (hi + k) % ratio)
            to_pair(s, c, k, l_slot(s, (hi + k) % ratio, c)).start()

    def rest_own(s):
        @pl.when(jnp.logical_not(owner))
        def _():
            half_arrived(s, hi)

    def rest(s):
        for k in range(1, ratio):
            half_arrived(s, (hi + k) % ratio)

    def drain_blocks(s):
        for k in range(1, ratio):
            half_sent(s, k - 1)
            half_sent(s, ratio - 1 + n_cols // 2 - 1 + k)

        @pl.when(source_chip)
        def _():
            for j in range(1, n_cols // 2):
                half_sent(s, ratio - 1 + j - 1)

        @pl.when(t != 1)
        def _():
            half_sent(s, ratio - 1 + n_cols // 2 - 1)

        @pl.when(owner)
        def _():
            half_sent(s, 2 * ratio - 1 + n_cols // 2 - 1)

    def choose(k):
        strip_copy(k).wait()
        if k + AHEAD < STRIPS:
            strip_copy(k + AHEAD).start()
        for s in range(nodes):
            for b in range(block // 128):
                lanes = raw[k][row[s], :, :, b * 128:(b + 1) * 128].astype(jnp.float32)
                wide[s, b] = lanes.reshape(strip * cols_local, 128)
            for h in range(ratio):
                for b in range(block // 128):
                    a_ref[s, h, k * strip:(k + 1) * strip, b * 128:(b + 1) * 128] = wide[
                        s, b, pl.ds(cols[s][h], strip, stride=cols_local)
                    ].astype(jnp.bfloat16)

    def multiply_own(s):
        rest_own(s)
        total = jnp.dot(a_ref[s, hi], l_buf[s, hi], preferred_element_type=jnp.float32)
        for d in range(n_cols):
            part[s, d] = total[d * piece:(d + 1) * piece]

    def multiply(s):
        h = [(hi + k) % ratio for k in range(1, ratio)]
        total = jnp.dot(a_ref[s, h[0]], l_buf[s, h[0]], preferred_element_type=jnp.float32)
        for k in h[1:]:
            total += jnp.dot(a_ref[s, k], l_buf[s, k], preferred_element_type=jnp.float32)
        total = jnp.concatenate([part[s, d] + total[d * piece:(d + 1) * piece] for d in range(n_cols)], axis=0)
        for d in range(n_cols):
            part[s, d] = total[d * piece:(d + 1) * piece]
        return total

    def encoded(value):
        largest = jnp.maximum(jnp.max(jnp.abs(value), axis=0, keepdims=True), 1e-30)
        whole = jnp.floor(value * (FULL / largest) + 0.5).astype(jnp.int32).astype(jnp.int16)
        return whole, largest * (1.0 / FULL)

    def decoded(whole, scale):
        return whole.astype(jnp.int32).astype(jnp.float32) * scale

    def diagonal_term(s, total):
        high = total.astype(jnp.bfloat16)
        low = (total - high.astype(jnp.float32)).astype(jnp.bfloat16)
        over_rows = (((0,), (0,)), ((), ()))
        product = lax.dot_general(l_ref[s], high, over_rows, preferred_element_type=jnp.float32)
        product += lax.dot_general(l_ref[s], low, over_rows, preferred_element_type=jnp.float32)
        whole, scale = encoded(product)
        term_scale[s] = scale
        for k in range(n_rows):
            term[s, k] = product[k * seg:(k + 1) * seg]
            term_buf[s, k] = whole[k * seg:(k + 1) * seg]

    class both:
        def __init__(self, src, src_scale, dst, dst_scale, send, recv, send_at, recv_at, to_p, to_q):
            self.copies = [
                remote(src, dst, send.at[(0, *send_at)], recv.at[(0, *recv_at)], to_p, to_q),
                remote(src_scale, dst_scale, send.at[(1, *send_at)], recv.at[(1, *recv_at)], to_p, to_q),
            ]

        def start(self):
            for copy in self.copies:
                copy.start()

        def wait_send(self):
            for copy in self.copies:
                copy.wait_send()

        def wait_recv(self):
            for copy in self.copies:
                copy.wait_recv()

    def right_copy(s, d):
        return both(right_buf.at[s, d], right_scale.at[s, d], right_buf.at[s, d], right_scale.at[s, d],
                    r_send, r_recv, (s,), (s, d), p, (q + 1) % n_cols)

    def left_copy(s, d, at):
        last = jnp.where(at == d, n_cols, d)
        return both(left_buf.at[s, d], left_scale.at[s, d], left_buf.at[s, d], left_scale.at[s, d],
                    f_send, r_recv, (s,), (s, last), p, (q + n_cols - 1) % n_cols)

    def right_send(s, d, value):
        right_buf[s, d], right_scale[s, d] = encoded(value)
        right_copy(s, d).start()

    def left_send(s, d, value):
        left_buf[s, d], left_scale[s, d] = encoded(value)
        left_copy(s, d, q - 1).start()

    def line_start(s, nearest):
        @pl.when(q == 0)
        def _():
            for d in ((1,) if nearest else range(n_cols - 1, 1, -1)):
                right_send(s, d, part[s, d])

        @pl.when(q == n_cols - 1)
        def _():
            for d in ((n_cols - 2,) if nearest else range(n_cols - 2)):
                left_send(s, d, part[s, d])

    def relay_right(s):
        for d in range(n_cols - 1, 1, -1):
            @pl.when(jnp.logical_and(q > 0, q < d))
            def _():
                right_copy(s, d).wait_recv()
                right_send(s, d, decoded(right_buf[s, d], right_scale[s, d]) + part[s, d])

    def relay_left(s):
        for e in range(n_cols - 2):
            @pl.when(jnp.logical_and(q < n_cols - 1, q > e))
            def _():
                left_copy(s, e, q).wait_recv()
                left_send(s, e, decoded(left_buf[s, e], left_scale[s, e]) + part[s, e])

    left_half = 2 * q < n_cols - 1

    def relay(s, first):
        @pl.when(left_half)
        def _():
            (relay_right if first else relay_left)(s)

        @pl.when(jnp.logical_not(left_half))
        def _():
            (relay_left if first else relay_right)(s)

    def near(s, source):
        @pl.when(source_chip if source else jnp.logical_not(source_chip))
        def _():
            line_start(s, True)

    def relay_early(s, source):
        @pl.when(source_chip if source else jnp.logical_not(source_chip))
        def _():
            relay(s, True)

    def line_finish(s):
        @pl.when(q > 0)
        def _():
            right_copy(s, q).wait_recv()
            part[s, q] = part[s, q] + decoded(right_buf[s, q], right_scale[s, q])

        @pl.when(q < n_cols - 1)
        def _():
            left_copy(s, q, q).wait_recv()
            part[s, q] = part[s, q] + decoded(left_buf[s, q], left_scale[s, q])

        y_ref[s] = (-part[s, q]).astype(jnp.bfloat16)
        pltpu.make_async_copy(y_ref.at[s], y_out.at[s], o_sem.at[s, 0]).start()

    def line_drain(s):
        for at in range(n_cols):
            @pl.when(q == at)
            def _():
                for n, buf, scale, send in ((n_cols - 1 - at, right_buf, right_scale, r_send),
                                            (at, left_buf, left_scale, f_send)):
                    if n:
                        some = pl.ds(0, n)
                        both(buf.at[s, some], scale.at[s, some], buf.at[s, some], scale.at[s, some],
                             send, r_recv, (s,), (s, 0), p, (q + 1) % n_cols).wait_send()

    def plane_copy(s, k):
        to = (p + k) % n_rows
        return both(term_buf.at[s, to], term_scale.at[s], plane_buf.at[s, n_rows - k], plane_scale.at[s, n_rows - k],
                    p_send, p_recv, (s,), (s,), to, q)

    def col_copy(s, k):
        to = (q + k) % n_cols
        return both(col_own.at[s], col_own_scale.at[s], col_buf.at[s, q], col_scale.at[s, q],
                    c_send, c_recv, (s,), (s,), p, to)

    def gath_copy(s, k):
        to = (p + k) % n_rows
        return both(own.at[s], own_scale.at[s], g_out.at[s, p], scale_out.at[s, p],
                    g_send, g_recv, (s,), (s,), to, q)

    def all_of(s, n, buf, scale, send, recv):
        some = pl.ds(0, n - 1)
        return both(buf.at[s, some], scale.at[s, some], buf.at[s, some], scale.at[s, some],
                    send, recv, (s,), (s,), pair, q)

    def plane_all(s):
        return all_of(s, n_rows, plane_buf, plane_scale, p_send, p_recv)

    def col_all(s):
        return all_of(s, n_cols, col_buf, col_scale, c_send, c_recv)

    def gath_all(s):
        return all_of(s, n_rows, g_out, scale_out, g_send, g_recv)

    def own_copies(s):
        return [pltpu.make_async_copy(own.at[s], g_out.at[s, p], o_sem.at[s, 1]),
                pltpu.make_async_copy(own_scale.at[s], scale_out.at[s, p], o_sem.at[s, 2])]

    def plane_start(s):
        for k in range(1, n_rows):
            plane_copy(s, k).start()

    def col_start(s):
        total = term[s, p]
        plane_all(s).wait_recv()
        for k in range(1, n_rows):
            total = total + decoded(plane_buf[s, k], plane_scale[s, k])
        col_own[s], col_own_scale[s] = encoded(total)
        for k in range(1, n_cols):
            col_copy(s, k).start()

    def gath_start(s):
        mine_own = decoded(col_own[s], col_own_scale[s])
        col_all(s).wait_recv()
        total = jnp.zeros_like(mine_own)
        for k in range(n_cols):
            total = total + jnp.where(q == k, mine_own, decoded(col_buf[s, k], col_scale[s, k]))
        own[s], own_scale[s] = encoded(total)
        for k in range(1, n_rows):
            gath_copy(s, k).start()
        for copy in own_copies(s):
            copy.start()

    def finish_diagonal(s):
        pltpu.make_async_copy(y_ref.at[s], y_out.at[s], o_sem.at[s, 0]).wait()
        for copy in own_copies(s):
            copy.wait()
        gath_all(s).wait_recv()

    def after(s, total):
        with scope(f"line{s}"):
            line_start(s, False)
            near(s, True)
        with scope(f"diag{s}"):
            diagonal_term(s, total)
            plane_start(s)

    with scope("frompair"):
        for s in range(nodes):
            for u in range(SUB):
                own_from_pair(s, u)
    def flow(s):
        order = []
        for u in range(SUB):
            order.append((others_from_hi, s, u))
            if s + 1 < nodes:
                order.append((own_from_x, s + 1, u))
        return order

    first = [(own_from_x, 0, u) for u in range(SUB)] + flow(0)
    chosen = 0
    for i, (step, s, u) in enumerate(first):
        ready = STRIPS if i + 1 == len(first) else min(STRIPS, 2 + i)
        with scope(f"choose{i}"):
            for k in range(chosen, ready):
                choose(k)
            chosen = ready
        if i + 2 == len(first):
            with scope("own0"):
                multiply_own(0)
        with scope(f"{step.__name__}{s}{u}"):
            step(s, u)
    for s in range(nodes):
        with scope(f"rest{s}"):
            rest(s)
        with scope(f"mult{s}"):
            total = multiply(s)
        after(s, total)
        if s + 1 < nodes:
            order = flow(s + 1)
            for i, (step, to, u) in enumerate(order):
                if 2 * i == len(order):
                    with scope(f"own{s + 1}"):
                        multiply_own(s + 1)
                with scope(f"flow{s + 1}{i}"):
                    step(to, u)
            with scope(f"relayA{s}"):
                relay_early(s, True)
    for s in range(nodes):
        if s + 1 < nodes:
            with scope(f"relayT{s}"):
                relay_early(s, False)
        with scope(f"colstart{s}"):
            col_start(s)
            near(s, False)
        if s + 1 == nodes:
            with scope(f"relayA{s}"):
                relay(s, True)
            for i in range(nodes - 1):
                with scope(f"gathstart{i}"):
                    gath_start(i)
        with scope(f"relayB{s}"):
            relay(s, False)
    with scope(f"gathstart{nodes - 1}"):
        gath_start(nodes - 1)
    for s in range(nodes):
        with scope(f"finish{s}"):
            line_finish(s)
    with scope("drain"):
        for s in range(nodes):
            drain_blocks(s)
            line_drain(s)
            plane_all(s).wait_send()
            col_all(s).wait_send()
    for s in range(nodes):
        with scope(f"findiag{s}"):
            finish_diagonal(s)
    for s in range(nodes):
        with scope("sent"):
            gath_all(s).wait_send()


def put_out(structure_ref, y_ref, whole_ref, scale_ref, d_ref, off_ref, out_ref, off_buf, out_buf, sem):
    nodes, n_rows, seg, _ = whole_ref.shape
    rows_local = off_ref.shape[1]
    copies = []
    for s in range(nodes):
        row = find_row(structure_ref, s, lax.axis_index("prow"), n_rows, n_rows)
        value = y_ref[s]
        for r in range(rows_local):
            off_buf[s, r] = jnp.where(row == r, value, jnp.zeros_like(value))
        copies.append(pltpu.make_async_copy(off_buf.at[s], off_ref.at[s], sem.at[0, s]))
        copies[-1].start()
        for k in range(n_rows):
            term = whole_ref[s, k].astype(jnp.int32).astype(jnp.float32) * scale_ref[s, k]
            out_buf[s, k * seg:(k + 1) * seg] = d_ref[s, k * seg:(k + 1) * seg] + term
        copies.append(pltpu.make_async_copy(out_buf.at[s], out_ref.at[s], sem.at[1, s]))
        copies[-1].start()
    for copy in copies:
        copy.wait()


def on_device(inverse, panel, structure, diag_inverse):
    n_rows = lax.axis_size("prow")
    n_cols = lax.axis_size("pcol")
    rows_local, block, cols_local, _ = inverse.shape
    nodes, _, _, width = panel.shape
    ratio = n_rows // n_cols
    piece = block // n_cols
    seg = width // n_rows
    strip = block // STRIPS

    vmem = pl.BlockSpec(memory_space=pltpu.VMEM)
    hbm = pl.BlockSpec(memory_space=pltpu.HBM)
    f32, bf16, i16 = jnp.float32, jnp.bfloat16, jnp.int16
    dma = pltpu.SemaphoreType.DMA
    sends = ratio + n_cols // 2 - 1 + ratio
    operands = [pltpu.with_memory_space_constraint(x, pltpu.HBM) for x in (structure, inverse, panel)]
    anywhere = pl.BlockSpec(memory_space=pl.ANY)
    smem = pl.BlockSpec(memory_space=pltpu.SMEM)
    pieces, whole, scale = pl.pallas_call(
        functools.partial(selected, n_rows, n_cols),
        out_shape=(
            jax.ShapeDtypeStruct((nodes, piece, width), bf16),
            jax.ShapeDtypeStruct((nodes, n_rows, seg, width), i16),
            jax.ShapeDtypeStruct((nodes, n_rows, 1, width), f32),
        ),
        in_specs=[hbm] * 3,
        out_specs=(anywhere, anywhere, anywhere),
        scratch_shapes=[
            pltpu.SMEM(structure.shape, jnp.int32),
            pltpu.VMEM((nodes, piece, width), bf16),
            pltpu.VMEM((nodes, seg, width), i16),
            pltpu.VMEM((nodes, 1, width), f32),
            tuple(pltpu.VMEM(panel.shape[1:], bf16) for _ in range(nodes)),
            tuple(pltpu.VMEM((rows_local, strip, *inverse.shape[2:]), bf16) for _ in range(STRIPS)),
            pltpu.VMEM((nodes, block // 128, strip * cols_local, 128), f32),
            pltpu.VMEM((nodes, ratio, block, block), bf16),
            pltpu.VMEM((nodes, block, width), bf16),
            pltpu.VMEM((nodes, ratio, block, width), bf16),
            pltpu.VMEM((nodes, n_cols, piece, width), f32),
            pltpu.VMEM((nodes, n_cols, piece, width), i16),
            pltpu.VMEM((nodes, n_cols, piece, width), i16),
            pltpu.VMEM((nodes, n_cols, 1, width), f32),
            pltpu.VMEM((nodes, n_cols, 1, width), f32),
            pltpu.VMEM((nodes, n_rows, seg, width), f32),
            pltpu.VMEM((nodes, n_rows, seg, width), i16),
            pltpu.VMEM((nodes, 1, width), f32),
            pltpu.VMEM((nodes, n_rows, seg, width), i16),
            pltpu.VMEM((nodes, n_rows, 1, width), f32),
            pltpu.VMEM((nodes, seg, width), i16),
            pltpu.VMEM((nodes, 1, width), f32),
            pltpu.VMEM((nodes, n_cols, seg, width), i16),
            pltpu.VMEM((nodes, n_cols, 1, width), f32),
            dma, dma((nodes,)), dma((AHEAD,)), dma((nodes, 3)),
            dma((nodes, sends)), dma((nodes, ratio, SUB + 1)),
            dma((2, nodes)), dma((2, nodes)), dma((2, nodes, n_cols + 1)),
            *(dma((2, nodes)) for _ in range(6)),
        ],
        compiler_params=pltpu.CompilerParams(
            collective_id=0, has_side_effects=True, vmem_limit_bytes=50 * 1024 * 1024
        ),
        name="selected_inverse",
    )(*operands)
    return pl.pallas_call(
        put_out,
        out_shape=(
            jax.ShapeDtypeStruct((nodes, rows_local, piece, width), bf16),
            jax.ShapeDtypeStruct(diag_inverse.shape, f32),
        ),
        in_specs=[smem, vmem, vmem, vmem, vmem],
        out_specs=(hbm, hbm),
        scratch_shapes=[
            pltpu.VMEM((nodes, rows_local, piece, width), bf16),
            pltpu.VMEM(diag_inverse.shape, f32),
            dma((2, nodes)),
        ],
        compiler_params=pltpu.CompilerParams(vmem_limit_bytes=4 * 1024 * 1024),
        name="put_out",
    )(structure, pieces, whole, scale, diag_inverse)


def solution(mesh):
    placed = (P(None, "prow", None, "pcol"), P(None, None, "prow", None), P(), P())
    return jax.shard_map(
        on_device,
        mesh=mesh,
        in_specs=placed,
        out_specs=(P(None, None, ("prow", "pcol"), None), P()),
        check_vma=False,
    )
```

```python
import functools

import jax
import jax.numpy as jnp
from jax import lax
from jax.experimental import pallas as pl
from jax.experimental.pallas import tpu as pltpu
from jax.sharding import PartitionSpec as P

MESH = pl.DeviceIdType.MESH
SUB = 4
STRIPS = 8
AHEAD = 4
FULL = 32700.0


def remote(src, dst, send, recv, p, q):
    return pltpu.make_async_remote_copy(
        src_ref=src, dst_ref=dst, send_sem=send, recv_sem=recv, device_id=(p, q), device_id_type=MESH
    )


def scope(name):
    return jax.named_scope(name)


def find_row(structure_ref, s, residue, n_rows, divisor):
    shift = divisor.bit_length() - 1
    found = jnp.int32(0)
    for i in range(structure_ref.shape[1]):
        value = structure_ref[s, i]
        found = found + jnp.where((value & (n_rows - 1)) == residue, value >> shift, 0)
    return found


def selected(
    n_rows, n_cols, structure_hbm, inverse_ref, panel_ref, y_out, g_out, scale_out, mask_out,
    structure_ref, mask, y_ref, own, own_scale, panel_buf, raw, wide, a_ref, l_ref, l_buf, part,
    right_buf, left_buf, right_scale, left_scale,
    term, term_buf, term_scale, plane_buf, plane_scale, col_own, col_own_scale, col_buf, col_scale,
    s_sem, m_sem, n_sem, a_sem, o_sem,
    l_send, l_recv, r_send, f_send, r_recv, p_send, p_recv, c_send, c_recv, g_send, g_recv,
):
    p = lax.axis_index("prow")
    q = lax.axis_index("pcol")
    nodes, ratio, block, width = l_buf.shape
    rows_local, _, cols_local, _ = inverse_ref.shape
    piece = block // n_cols
    seg = width // n_rows
    chunk = block // (2 * SUB)
    strip = block // STRIPS
    hi = p // n_cols
    lo = p % n_cols
    t = jnp.int32(0)
    bit = 1
    while bit < n_cols:
        t = t + bit * (((lo // bit) + (q // bit)) % 2)
        bit *= 2
    pair = p + 1 - 2 * (p % 2)

    def beside(j):
        lo2 = jnp.int32(0)
        b = 1
        while b < n_cols:
            lo2 = lo2 + b * (((lo // b) + (2 * j // b)) % 2)
            b *= 2
        return hi * n_cols + lo2

    structure_copy = pltpu.make_async_copy(structure_hbm, structure_ref, s_sem)
    structure_copy.start()
    panel_copies = [pltpu.make_async_copy(panel_ref.at[s], panel_buf[s], n_sem.at[s]) for s in range(nodes)]
    for copy in panel_copies:
        copy.start()

    def strip_copy(k):
        part_of = pl.ds(k * strip, strip)
        return pltpu.make_async_copy(inverse_ref.at[:, part_of], raw[k], a_sem.at[k % AHEAD])

    barrier = pltpu.get_barrier_semaphore()
    for k in range(1, n_rows):
        pl.semaphore_signal(barrier, inc=1, device_id=((p + k) % n_rows, q), device_id_type=MESH)
    for k in range(1, n_cols):
        pl.semaphore_signal(barrier, inc=1, device_id=(p, (q + k) % n_cols), device_id_type=MESH)

    def find(s, residue, divisor):
        return find_row(structure_ref, s, residue, n_rows, divisor)

    with scope("pickl"):
        structure_copy.wait()
        row = [find(0, p, n_rows)]
        panel_copies[0].wait()
        l_ref[0] = panel_buf[0][row[0]]
        for k in range(AHEAD):
            strip_copy(k).start()

    with scope("barrier"):
        pl.semaphore_wait(barrier, n_rows + n_cols - 2)

    def rows(c):
        return pl.ds(pl.multiple_of(c * chunk, chunk), chunk)

    def l_slot(s, h, c):
        return l_buf.at[s, h, rows(c)]

    def to_peer_hi(s, c, k, src):
        return remote(src, l_slot(s, hi, c), l_send.at[s, k - 1], l_recv.at[s, hi, c % SUB],
                      (p + k * n_cols) % n_rows, q)

    def to_x(s, c, j, src):
        return remote(src, l_slot(s, hi, c), l_send.at[s, ratio - 1 + j - 1], l_recv.at[s, hi, c % SUB],
                      beside(j), q)

    def to_pair(s, c, k, src):
        h = (hi + k) % ratio
        return remote(src, l_slot(s, h, c), l_send.at[s, ratio - 1 + n_cols // 2 - 1 + k],
                      l_recv.at[s, h, SUB], pair, q)

    def hand_over(s, c):
        return remote(l_ref.at[s, rows(c)], l_slot(s, hi, c), l_send.at[s, 2 * ratio - 1 + n_cols // 2 - 1],
                      l_recv.at[s, hi, c % SUB], pair, q)

    def l_arrived(s, c, h):
        remote(l_slot(s, h, c), l_slot(s, h, c), l_send.at[s, 0], l_recv.at[s, h, c % SUB], pair, q).wait_recv()

    def half(s, h):
        return l_buf.at[s, h, pl.ds(0, SUB * chunk)]

    def half_arrived(s, h):
        remote(half(s, h), half(s, h), l_send.at[s, 0], l_recv.at[s, h, SUB], pair, q).wait_recv()

    def half_sent(s, i):
        remote(half(s, 0), half(s, 0), l_send.at[s, i], l_recv.at[s, 0, 0], pair, q).wait_send()

    owner = t == 0
    source_chip = t < 2
    core = p % 2

    def mine(u):
        return core * SUB + u

    def other(u):
        return (1 - core) * SUB + u

    for s in range(nodes):
        if s > 0:
            row.append(find(s, p, n_rows))
            panel_copies[s].wait()
            l_ref[s] = panel_buf[s][row[s]]

        @pl.when(owner)
        def _():
            for u in range(SUB):
                hand_over(s, other(u)).start()
            for u in range(SUB):
                src = l_ref.at[s, rows(mine(u))]
                for j in range(1, n_cols // 2):
                    to_x(s, mine(u), j, src).start()
                for k in range(1, ratio):
                    to_peer_hi(s, mine(u), k, src).start()
            for u in range(SUB):
                to_pair(s, mine(u), 0, l_ref.at[s, rows(mine(u))]).start()

    cols = [[find(s, h * n_cols + q, n_cols) for h in range(ratio)] for s in range(nodes)]
    for s in range(nodes):
        for r in range(rows_local):
            mask[s, r] = jnp.broadcast_to(jnp.where(row[s] == r, 1.0, 0.0), mask.shape[2:])
    mask_copy = pltpu.make_async_copy(mask, mask_out, m_sem)
    mask_copy.start()

    @pl.when(owner)
    def _():
        for s in range(nodes):
            l_buf[s, hi] = l_ref[s]

    def own_from_pair(s, u):
        c = mine(u)

        @pl.when(t == 1)
        def _():
            l_arrived(s, c, hi)
            for j in range(1, n_cols // 2):
                to_x(s, c, j, l_slot(s, hi, c)).start()
            for k in range(1, ratio):
                to_peer_hi(s, c, k, l_slot(s, hi, c)).start()

    def own_from_x(s, u):
        c = mine(u)

        @pl.when(jnp.logical_not(source_chip))
        def _():
            l_arrived(s, c, hi)
            for k in range(1, ratio):
                to_peer_hi(s, c, k, l_slot(s, hi, c)).start()
            to_pair(s, c, 0, l_slot(s, hi, c)).start()

    def others_from_hi(s, u):
        c = mine(u)
        for k in range(1, ratio):
            l_arrived(s, c, (hi + k) % ratio)
            to_pair(s, c, k, l_slot(s, (hi + k) % ratio, c)).start()

    def rest_own(s):
        @pl.when(jnp.logical_not(owner))
        def _():
            half_arrived(s, hi)

    def rest(s):
        for k in range(1, ratio):
            half_arrived(s, (hi + k) % ratio)

    def drain_blocks(s):
        for k in range(1, ratio):
            half_sent(s, k - 1)
            half_sent(s, ratio - 1 + n_cols // 2 - 1 + k)

        @pl.when(source_chip)
        def _():
            for j in range(1, n_cols // 2):
                half_sent(s, ratio - 1 + j - 1)

        @pl.when(t != 1)
        def _():
            half_sent(s, ratio - 1 + n_cols // 2 - 1)

        @pl.when(owner)
        def _():
            half_sent(s, 2 * ratio - 1 + n_cols // 2 - 1)

    def choose(k):
        strip_copy(k).wait()
        if k + AHEAD < STRIPS:
            strip_copy(k + AHEAD).start()
        for s in range(nodes):
            for b in range(block // 128):
                lanes = raw[k][row[s], :, :, b * 128:(b + 1) * 128].astype(jnp.float32)
                wide[s, b] = lanes.reshape(strip * cols_local, 128)
            for h in range(ratio):
                for b in range(block // 128):
                    a_ref[s, h, k * strip:(k + 1) * strip, b * 128:(b + 1) * 128] = wide[
                        s, b, pl.ds(cols[s][h], strip, stride=cols_local)
                    ].astype(jnp.bfloat16)

    def multiply_own(s):
        rest_own(s)
        total = jnp.dot(a_ref[s, hi], l_buf[s, hi], preferred_element_type=jnp.float32)
        for d in range(n_cols):
            part[s, d] = total[d * piece:(d + 1) * piece]

    def multiply(s):
        h = [(hi + k) % ratio for k in range(1, ratio)]
        total = jnp.dot(a_ref[s, h[0]], l_buf[s, h[0]], preferred_element_type=jnp.float32)
        for k in h[1:]:
            total += jnp.dot(a_ref[s, k], l_buf[s, k], preferred_element_type=jnp.float32)
        total = jnp.concatenate([part[s, d] + total[d * piece:(d + 1) * piece] for d in range(n_cols)], axis=0)
        for d in range(n_cols):
            part[s, d] = total[d * piece:(d + 1) * piece]
        return total

    def encoded(value):
        largest = jnp.maximum(jnp.max(jnp.abs(value), axis=0, keepdims=True), 1e-30)
        whole = jnp.floor(value * (FULL / largest) + 0.5).astype(jnp.int32).astype(jnp.int16)
        return whole, largest * (1.0 / FULL)

    def decoded(whole, scale):
        return whole.astype(jnp.int32).astype(jnp.float32) * scale

    def diagonal_term(s, total):
        high = total.astype(jnp.bfloat16)
        low = (total - high.astype(jnp.float32)).astype(jnp.bfloat16)
        over_rows = (((0,), (0,)), ((), ()))
        product = lax.dot_general(l_ref[s], high, over_rows, preferred_element_type=jnp.float32)
        product += lax.dot_general(l_ref[s], low, over_rows, preferred_element_type=jnp.float32)
        whole, scale = encoded(product)
        term_scale[s] = scale
        for k in range(n_rows):
            term[s, k] = product[k * seg:(k + 1) * seg]
            term_buf[s, k] = whole[k * seg:(k + 1) * seg]

    class both:
        def __init__(self, src, src_scale, dst, dst_scale, send, recv, send_at, recv_at, to_p, to_q):
            self.copies = [
                remote(src, dst, send.at[(0, *send_at)], recv.at[(0, *recv_at)], to_p, to_q),
                remote(src_scale, dst_scale, send.at[(1, *send_at)], recv.at[(1, *recv_at)], to_p, to_q),
            ]

        def start(self):
            for copy in self.copies:
                copy.start()

        def wait_send(self):
            for copy in self.copies:
                copy.wait_send()

        def wait_recv(self):
            for copy in self.copies:
                copy.wait_recv()

    def right_copy(s, d):
        return both(right_buf.at[s, d], right_scale.at[s, d], right_buf.at[s, d], right_scale.at[s, d],
                    r_send, r_recv, (s,), (s, d), p, (q + 1) % n_cols)

    def left_copy(s, d, at):
        last = jnp.where(at == d, n_cols, d)
        return both(left_buf.at[s, d], left_scale.at[s, d], left_buf.at[s, d], left_scale.at[s, d],
                    f_send, r_recv, (s,), (s, last), p, (q + n_cols - 1) % n_cols)

    def right_send(s, d, value):
        right_buf[s, d], right_scale[s, d] = encoded(value)
        right_copy(s, d).start()

    def left_send(s, d, value):
        left_buf[s, d], left_scale[s, d] = encoded(value)
        left_copy(s, d, q - 1).start()

    def line_start(s, nearest):
        @pl.when(q == 0)
        def _():
            for d in ((1,) if nearest else range(n_cols - 1, 1, -1)):
                right_send(s, d, part[s, d])

        @pl.when(q == n_cols - 1)
        def _():
            for d in ((n_cols - 2,) if nearest else range(n_cols - 2)):
                left_send(s, d, part[s, d])

    def relay_right(s, some=slice(None)):
        for d in range(n_cols - 1, 1, -1)[some]:
            @pl.when(jnp.logical_and(q > 0, q < d))
            def _():
                right_copy(s, d).wait_recv()
                right_send(s, d, decoded(right_buf[s, d], right_scale[s, d]) + part[s, d])

    def relay_left(s, some=slice(None)):
        for e in range(n_cols - 2)[some]:
            @pl.when(jnp.logical_and(q < n_cols - 1, q > e))
            def _():
                left_copy(s, e, q).wait_recv()
                left_send(s, e, decoded(left_buf[s, e], left_scale[s, e]) + part[s, e])

    left_half = 2 * q < n_cols - 1

    def relay(s, first, some=slice(None)):
        @pl.when(left_half)
        def _():
            (relay_right if first else relay_left)(s, some)

        @pl.when(jnp.logical_not(left_half))
        def _():
            (relay_left if first else relay_right)(s, some)

    def near(s, source):
        @pl.when(source_chip if source else jnp.logical_not(source_chip))
        def _():
            line_start(s, True)

    def relay_early(s, source, some=slice(None)):
        @pl.when(source_chip if source else jnp.logical_not(source_chip))
        def _():
            relay(s, True, some)

    def line_finish(s):
        @pl.when(q > 0)
        def _():
            right_copy(s, q).wait_recv()
            part[s, q] = part[s, q] + decoded(right_buf[s, q], right_scale[s, q])

        @pl.when(q < n_cols - 1)
        def _():
            left_copy(s, q, q).wait_recv()
            part[s, q] = part[s, q] + decoded(left_buf[s, q], left_scale[s, q])

        y_ref[s] = (-part[s, q]).astype(jnp.bfloat16)
        pltpu.make_async_copy(y_ref.at[s], y_out.at[s], o_sem.at[s, 0]).start()

    def line_drain(s):
        for at in range(n_cols):
            @pl.when(q == at)
            def _():
                for n, buf, scale, send in ((n_cols - 1 - at, right_buf, right_scale, r_send),
                                            (at, left_buf, left_scale, f_send)):
                    if n:
                        some = pl.ds(0, n)
                        both(buf.at[s, some], scale.at[s, some], buf.at[s, some], scale.at[s, some],
                             send, r_recv, (s,), (s, 0), p, (q + 1) % n_cols).wait_send()

    def plane_copy(s, k):
        to = (p + k) % n_rows
        return both(term_buf.at[s, to], term_scale.at[s], plane_buf.at[s, n_rows - k], plane_scale.at[s, n_rows - k],
                    p_send, p_recv, (s,), (s,), to, q)

    def col_copy(s, k):
        to = (q + k) % n_cols
        return both(col_own.at[s], col_own_scale.at[s], col_buf.at[s, q], col_scale.at[s, q],
                    c_send, c_recv, (s,), (s,), p, to)

    def gath_copy(s, k):
        to = (p + k) % n_rows
        return both(own.at[s], own_scale.at[s], g_out.at[s, p], scale_out.at[s, p],
                    g_send, g_recv, (s,), (s,), to, q)

    def all_of(s, n, buf, scale, send, recv):
        some = pl.ds(0, n - 1)
        return both(buf.at[s, some], scale.at[s, some], buf.at[s, some], scale.at[s, some],
                    send, recv, (s,), (s,), pair, q)

    def plane_all(s):
        return all_of(s, n_rows, plane_buf, plane_scale, p_send, p_recv)

    def col_all(s):
        return all_of(s, n_cols, col_buf, col_scale, c_send, c_recv)

    def gath_all(s):
        return all_of(s, n_rows, g_out, scale_out, g_send, g_recv)

    def own_copies(s):
        return [pltpu.make_async_copy(own.at[s], g_out.at[s, p], o_sem.at[s, 1]),
                pltpu.make_async_copy(own_scale.at[s], scale_out.at[s, p], o_sem.at[s, 2])]

    def plane_start(s):
        for k in range(1, n_rows):
            plane_copy(s, k).start()

    def col_start(s):
        total = term[s, p]
        plane_all(s).wait_recv()
        for k in range(1, n_rows):
            total = total + decoded(plane_buf[s, k], plane_scale[s, k])
        col_own[s], col_own_scale[s] = encoded(total)
        for k in range(1, n_cols):
            col_copy(s, k).start()

    def gath_start(s):
        mine_own = decoded(col_own[s], col_own_scale[s])
        col_all(s).wait_recv()
        total = jnp.zeros_like(mine_own)
        for k in range(n_cols):
            total = total + jnp.where(q == k, mine_own, decoded(col_buf[s, k], col_scale[s, k]))
        own[s], own_scale[s] = encoded(total)
        for k in range(1, n_rows):
            gath_copy(s, k).start()
        for copy in own_copies(s):
            copy.start()

    def finish_diagonal(s):
        pltpu.make_async_copy(y_ref.at[s], y_out.at[s], o_sem.at[s, 0]).wait()
        for copy in own_copies(s):
            copy.wait()
        gath_all(s).wait_recv()

    def after(s, total):
        with scope(f"line{s}"):
            line_start(s, False)
            if s + 1 == nodes:
                for i in range(nodes):
                    near(i, True)
        with scope(f"diag{s}"):
            diagonal_term(s, total)
            plane_start(s)

    with scope("frompair"):
        for s in range(nodes):
            for u in range(SUB):
                own_from_pair(s, u)
    def flow(s):
        order = []
        for u in range(SUB):
            order.append((others_from_hi, s, u))
            if s + 1 < nodes:
                order.append((own_from_x, s + 1, u))
        return order

    first = [(own_from_x, 0, u) for u in range(SUB)] + flow(0)
    chosen = 0
    for i, (step, s, u) in enumerate(first):
        ready = STRIPS if i + 1 == len(first) else min(STRIPS, 2 + i)
        with scope(f"choose{i}"):
            for k in range(chosen, ready):
                choose(k)
            chosen = ready
        if i + 2 == len(first):
            with scope("own0"):
                multiply_own(0)
        with scope(f"{step.__name__}{s}{u}"):
            step(s, u)
    for s in range(nodes):
        with scope(f"rest{s}"):
            rest(s)
        with scope(f"mult{s}"):
            total = multiply(s)
        after(s, total)
        if s + 1 < nodes:
            order = flow(s + 1)
            for i, (step, to, u) in enumerate(order):
                if 2 * i == len(order):
                    with scope(f"own{s + 1}"):
                        multiply_own(s + 1)
                with scope(f"flow{s + 1}{i}"):
                    step(to, u)
            with scope(f"relayA{s}"):
                relay_early(s, True)
    last = nodes - 1
    for s in range(last):
        with scope(f"relayT{s}"):
            relay_early(s, False)
    for s in range(nodes):
        with scope(f"colstart{s}"):
            col_start(s)
        if s < last:
            with scope(f"relayA{s + 1}"):
                relay_early(s + 1, True)
            with scope(f"relayB{s}"):
                relay(s, False)
    for s in range(nodes):
        near(s, False)
    with scope(f"relayT{last}"):
        relay_early(last, False, slice(0, 1))
    for s in range(last):
        with scope(f"gathstart{s}"):
            gath_start(s)
    with scope(f"relayU{last}"):
        relay_early(last, False, slice(1, None))
    with scope(f"gathstart{last}"):
        gath_start(last)
    with scope(f"relayB{last}"):
        relay(last, False)
    for s in range(nodes):
        with scope(f"finish{s}"):
            line_finish(s)
    with scope("drain"):
        mask_copy.wait()
        for s in range(nodes):
            drain_blocks(s)
            line_drain(s)
            plane_all(s).wait_send()
            col_all(s).wait_send()
    for s in range(nodes):
        with scope(f"findiag{s}"):
            finish_diagonal(s)
    for s in range(nodes):
        with scope("sent"):
            gath_all(s).wait_send()


def put_out(mask_ref, y_ref, whole_ref, scale_ref, d_ref, off_ref, out_ref, off_buf, out_buf, sem):
    nodes, n_rows, seg, _ = whole_ref.shape
    copies = []
    for s in range(nodes):
        value = y_ref[s].astype(jnp.float32)
        for r in range(off_ref.shape[1]):
            off_buf[s, r] = jnp.where(mask_ref[s, r] > 0, value, 0.0).astype(jnp.bfloat16)
        copies.append(pltpu.make_async_copy(off_buf.at[s], off_ref.at[s], sem.at[0, s]))
        copies[-1].start()
        for k in range(n_rows):
            term = whole_ref[s, k].astype(jnp.int32).astype(jnp.float32) * scale_ref[s, k]
            out_buf[s, k * seg:(k + 1) * seg] = d_ref[s, k * seg:(k + 1) * seg] + term
        copies.append(pltpu.make_async_copy(out_buf.at[s], out_ref.at[s], sem.at[1, s]))
        copies[-1].start()
    for copy in copies:
        copy.wait()


def on_device(inverse, panel, structure, diag_inverse):
    n_rows = lax.axis_size("prow")
    n_cols = lax.axis_size("pcol")
    rows_local, block, cols_local, _ = inverse.shape
    nodes, _, _, width = panel.shape
    ratio = n_rows // n_cols
    piece = block // n_cols
    seg = width // n_rows
    strip = block // STRIPS

    vmem = pl.BlockSpec(memory_space=pltpu.VMEM)
    hbm = pl.BlockSpec(memory_space=pltpu.HBM)
    f32, bf16, i16 = jnp.float32, jnp.bfloat16, jnp.int16
    dma = pltpu.SemaphoreType.DMA
    sends = ratio + n_cols // 2 - 1 + ratio
    operands = [pltpu.with_memory_space_constraint(x, pltpu.HBM) for x in (structure, inverse, panel)]
    anywhere = pl.BlockSpec(memory_space=pl.ANY)
    pieces, whole, scale, mask = pl.pallas_call(
        functools.partial(selected, n_rows, n_cols),
        out_shape=(
            jax.ShapeDtypeStruct((nodes, piece, width), bf16),
            jax.ShapeDtypeStruct((nodes, n_rows, seg, width), i16),
            jax.ShapeDtypeStruct((nodes, n_rows, 1, width), f32),
            jax.ShapeDtypeStruct((nodes, rows_local, 1, width), f32),
        ),
        in_specs=[hbm] * 3,
        out_specs=(anywhere,) * 4,
        scratch_shapes=[
            pltpu.SMEM(structure.shape, jnp.int32),
            pltpu.VMEM((nodes, rows_local, 1, width), f32),
            pltpu.VMEM((nodes, piece, width), bf16),
            pltpu.VMEM((nodes, seg, width), i16),
            pltpu.VMEM((nodes, 1, width), f32),
            tuple(pltpu.VMEM(panel.shape[1:], bf16) for _ in range(nodes)),
            tuple(pltpu.VMEM((rows_local, strip, *inverse.shape[2:]), bf16) for _ in range(STRIPS)),
            pltpu.VMEM((nodes, block // 128, strip * cols_local, 128), f32),
            pltpu.VMEM((nodes, ratio, block, block), bf16),
            pltpu.VMEM((nodes, block, width), bf16),
            pltpu.VMEM((nodes, ratio, block, width), bf16),
            pltpu.VMEM((nodes, n_cols, piece, width), f32),
            pltpu.VMEM((nodes, n_cols, piece, width), i16),
            pltpu.VMEM((nodes, n_cols, piece, width), i16),
            pltpu.VMEM((nodes, n_cols, 1, width), f32),
            pltpu.VMEM((nodes, n_cols, 1, width), f32),
            pltpu.VMEM((nodes, n_rows, seg, width), f32),
            pltpu.VMEM((nodes, n_rows, seg, width), i16),
            pltpu.VMEM((nodes, 1, width), f32),
            pltpu.VMEM((nodes, n_rows, seg, width), i16),
            pltpu.VMEM((nodes, n_rows, 1, width), f32),
            pltpu.VMEM((nodes, seg, width), i16),
            pltpu.VMEM((nodes, 1, width), f32),
            pltpu.VMEM((nodes, n_cols, seg, width), i16),
            pltpu.VMEM((nodes, n_cols, 1, width), f32),
            dma, dma, dma((nodes,)), dma((AHEAD,)), dma((nodes, 3)),
            dma((nodes, sends)), dma((nodes, ratio, SUB + 1)),
            dma((2, nodes)), dma((2, nodes)), dma((2, nodes, n_cols + 1)),
            *(dma((2, nodes)) for _ in range(6)),
        ],
        compiler_params=pltpu.CompilerParams(
            collective_id=0, has_side_effects=True, vmem_limit_bytes=50 * 1024 * 1024
        ),
        name="selected_inverse",
    )(*operands)
    return pl.pallas_call(
        put_out,
        out_shape=(
            jax.ShapeDtypeStruct((nodes, rows_local, piece, width), bf16),
            jax.ShapeDtypeStruct(diag_inverse.shape, f32),
        ),
        in_specs=[vmem] * 5,
        out_specs=(hbm, hbm),
        scratch_shapes=[
            pltpu.VMEM((nodes, rows_local, piece, width), bf16),
            pltpu.VMEM(diag_inverse.shape, f32),
            dma((2, nodes)),
        ],
        compiler_params=pltpu.CompilerParams(vmem_limit_bytes=4 * 1024 * 1024),
        name="put_out",
    )(mask, pieces, whole, scale, diag_inverse)


def solution(mesh):
    placed = (P(None, "prow", None, "pcol"), P(None, None, "prow", None), P(), P())
    return jax.shard_map(
        on_device,
        mesh=mesh,
        in_specs=placed,
        out_specs=(P(None, None, ("prow", "pcol"), None), P()),
        check_vma=False,
    )
```

```python
import functools

import jax
import jax.numpy as jnp
from jax import lax
from jax.experimental import pallas as pl
from jax.experimental.pallas import tpu as pltpu
from jax.sharding import PartitionSpec as P

MESH = pl.DeviceIdType.MESH
SUB = 8
STRIPS = 8
AHEAD = 4
FULL = 32700.0


def remote(src, dst, send, recv, p, q):
    return pltpu.make_async_remote_copy(
        src_ref=src, dst_ref=dst, send_sem=send, recv_sem=recv, device_id=(p, q), device_id_type=MESH
    )


def scope(name):
    return jax.named_scope(name)


def find_row(structure_ref, s, residue, n_rows, divisor):
    shift = divisor.bit_length() - 1
    found = jnp.int32(0)
    for i in range(structure_ref.shape[1]):
        value = structure_ref[s, i]
        found = found + jnp.where((value & (n_rows - 1)) == residue, value >> shift, 0)
    return found


def selected(
    n_rows, n_cols, structure_hbm, inverse_ref, panel_ref, y_out, g_out, scale_out, mask_out,
    structure_ref, mask, y_ref, own, own_scale, panel_buf, raw, wide, a_ref, l_ref, l_buf, part,
    right_buf, left_buf, right_scale, left_scale,
    term, term_buf, term_scale, plane_buf, plane_scale, col_own, col_own_scale, col_buf, col_scale,
    s_sem, m_sem, n_sem, a_sem, o_sem,
    l_send, l_recv, r_send, f_send, r_recv, p_send, p_recv, c_send, c_recv, g_send, g_recv,
):
    p = lax.axis_index("prow")
    q = lax.axis_index("pcol")
    nodes, ratio, block, width = l_buf.shape
    rows_local, _, cols_local, _ = inverse_ref.shape
    piece = block // n_cols
    seg = width // n_rows
    chunk = block // (2 * SUB)
    strip = block // STRIPS
    hi = p // n_cols
    lo = p % n_cols
    t = jnp.int32(0)
    bit = 1
    while bit < n_cols:
        t = t + bit * (((lo // bit) + (q // bit)) % 2)
        bit *= 2
    pair = p + 1 - 2 * (p % 2)

    def beside(j):
        lo2 = jnp.int32(0)
        b = 1
        while b < n_cols:
            lo2 = lo2 + b * (((lo // b) + (2 * j // b)) % 2)
            b *= 2
        return hi * n_cols + lo2

    structure_copy = pltpu.make_async_copy(structure_hbm, structure_ref, s_sem)
    structure_copy.start()
    panel_copies = [pltpu.make_async_copy(panel_ref.at[s], panel_buf[s], n_sem.at[s]) for s in range(nodes)]
    for copy in panel_copies:
        copy.start()

    def strip_copy(k):
        part_of = pl.ds(k * strip, strip)
        return pltpu.make_async_copy(inverse_ref.at[:, part_of], raw[k], a_sem.at[k % AHEAD])

    barrier = pltpu.get_barrier_semaphore()
    for k in range(1, n_rows):
        pl.semaphore_signal(barrier, inc=1, device_id=((p + k) % n_rows, q), device_id_type=MESH)
    for k in range(1, n_cols):
        pl.semaphore_signal(barrier, inc=1, device_id=(p, (q + k) % n_cols), device_id_type=MESH)

    def find(s, residue, divisor):
        return find_row(structure_ref, s, residue, n_rows, divisor)

    with scope("pickl"):
        structure_copy.wait()
        row = [find(0, p, n_rows)]
        panel_copies[0].wait()
        l_ref[0] = panel_buf[0][row[0]]
        for k in range(AHEAD):
            strip_copy(k).start()

    with scope("barrier"):
        pl.semaphore_wait(barrier, n_rows + n_cols - 2)

    def rows(c):
        return pl.ds(pl.multiple_of(c * chunk, chunk), chunk)

    def l_slot(s, h, c):
        return l_buf.at[s, h, rows(c)]

    def to_peer_hi(s, c, k, src):
        return remote(src, l_slot(s, hi, c), l_send.at[s, k - 1], l_recv.at[s, hi, c % SUB],
                      (p + k * n_cols) % n_rows, q)

    def to_x(s, c, j, src):
        return remote(src, l_slot(s, hi, c), l_send.at[s, ratio - 1 + j - 1], l_recv.at[s, hi, c % SUB],
                      beside(j), q)

    def to_pair(s, c, k, src):
        h = (hi + k) % ratio
        return remote(src, l_slot(s, h, c), l_send.at[s, ratio - 1 + n_cols // 2 - 1 + k],
                      l_recv.at[s, h, SUB], pair, q)

    def hand_over(s, c):
        return remote(l_ref.at[s, rows(c)], l_slot(s, hi, c), l_send.at[s, 2 * ratio - 1 + n_cols // 2 - 1],
                      l_recv.at[s, hi, c % SUB], pair, q)

    def l_arrived(s, c, h):
        remote(l_slot(s, h, c), l_slot(s, h, c), l_send.at[s, 0], l_recv.at[s, h, c % SUB], pair, q).wait_recv()

    def half(s, h):
        return l_buf.at[s, h, pl.ds(0, SUB * chunk)]

    def half_arrived(s, h):
        remote(half(s, h), half(s, h), l_send.at[s, 0], l_recv.at[s, h, SUB], pair, q).wait_recv()

    def half_sent(s, i):
        remote(half(s, 0), half(s, 0), l_send.at[s, i], l_recv.at[s, 0, 0], pair, q).wait_send()

    owner = t == 0
    source_chip = t < 2
    core = p % 2

    def mine(u):
        return core * SUB + u

    def other(u):
        return (1 - core) * SUB + u

    for s in range(nodes):
        if s > 0:
            row.append(find(s, p, n_rows))
            panel_copies[s].wait()
            l_ref[s] = panel_buf[s][row[s]]

        @pl.when(owner)
        def _():
            for u in range(SUB):
                hand_over(s, other(u)).start()
            for u in range(SUB):
                src = l_ref.at[s, rows(mine(u))]
                for j in range(1, n_cols // 2):
                    to_x(s, mine(u), j, src).start()
                for k in range(1, ratio):
                    to_peer_hi(s, mine(u), k, src).start()
            for u in range(SUB):
                to_pair(s, mine(u), 0, l_ref.at[s, rows(mine(u))]).start()

    cols = [[find(s, h * n_cols + q, n_cols) for h in range(ratio)] for s in range(nodes)]
    for s in range(nodes):
        for r in range(rows_local):
            mask[s, r] = jnp.broadcast_to(jnp.where(row[s] == r, 1.0, 0.0), mask.shape[2:])
    mask_copy = pltpu.make_async_copy(mask, mask_out, m_sem)
    mask_copy.start()

    @pl.when(owner)
    def _():
        for s in range(nodes):
            l_buf[s, hi] = l_ref[s]

    def own_from_pair(s, u):
        c = mine(u)

        @pl.when(t == 1)
        def _():
            l_arrived(s, c, hi)
            for j in range(1, n_cols // 2):
                to_x(s, c, j, l_slot(s, hi, c)).start()
            for k in range(1, ratio):
                to_peer_hi(s, c, k, l_slot(s, hi, c)).start()

    def own_from_x(s, u):
        c = mine(u)

        @pl.when(jnp.logical_not(source_chip))
        def _():
            l_arrived(s, c, hi)
            for k in range(1, ratio):
                to_peer_hi(s, c, k, l_slot(s, hi, c)).start()
            to_pair(s, c, 0, l_slot(s, hi, c)).start()

    def others_from_hi(s, u):
        c = mine(u)
        for k in range(1, ratio):
            l_arrived(s, c, (hi + k) % ratio)
            to_pair(s, c, k, l_slot(s, (hi + k) % ratio, c)).start()

    def rest_own(s):
        @pl.when(jnp.logical_not(owner))
        def _():
            half_arrived(s, hi)

    def rest(s):
        for k in range(1, ratio):
            half_arrived(s, (hi + k) % ratio)

    def drain_blocks(s):
        for k in range(1, ratio):
            half_sent(s, k - 1)
            half_sent(s, ratio - 1 + n_cols // 2 - 1 + k)

        @pl.when(source_chip)
        def _():
            for j in range(1, n_cols // 2):
                half_sent(s, ratio - 1 + j - 1)

        @pl.when(t != 1)
        def _():
            half_sent(s, ratio - 1 + n_cols // 2 - 1)

        @pl.when(owner)
        def _():
            half_sent(s, 2 * ratio - 1 + n_cols // 2 - 1)

    def choose(k):
        strip_copy(k).wait()
        if k + AHEAD < STRIPS:
            strip_copy(k + AHEAD).start()
        for s in range(nodes):
            for b in range(block // 128):
                lanes = raw[k][row[s], :, :, b * 128:(b + 1) * 128].astype(jnp.float32)
                wide[s, b] = lanes.reshape(strip * cols_local, 128)
            for h in range(ratio):
                for b in range(block // 128):
                    a_ref[s, h, k * strip:(k + 1) * strip, b * 128:(b + 1) * 128] = wide[
                        s, b, pl.ds(cols[s][h], strip, stride=cols_local)
                    ].astype(jnp.bfloat16)

    def multiply_own(s):
        rest_own(s)
        total = jnp.dot(a_ref[s, hi], l_buf[s, hi], preferred_element_type=jnp.float32)
        for d in range(n_cols):
            part[s, d] = total[d * piece:(d + 1) * piece]

    def multiply(s):
        h = [(hi + k) % ratio for k in range(1, ratio)]
        total = jnp.dot(a_ref[s, h[0]], l_buf[s, h[0]], preferred_element_type=jnp.float32)
        for k in h[1:]:
            total += jnp.dot(a_ref[s, k], l_buf[s, k], preferred_element_type=jnp.float32)
        total = jnp.concatenate([part[s, d] + total[d * piece:(d + 1) * piece] for d in range(n_cols)], axis=0)
        for d in range(n_cols):
            part[s, d] = total[d * piece:(d + 1) * piece]
        return total

    def encoded(value):
        largest = jnp.maximum(jnp.max(jnp.abs(value), axis=0, keepdims=True), 1e-30)
        whole = jnp.floor(value * (FULL / largest) + 0.5).astype(jnp.int32).astype(jnp.int16)
        return whole, largest * (1.0 / FULL)

    def decoded(whole, scale):
        return whole.astype(jnp.int32).astype(jnp.float32) * scale

    def diagonal_term(s, total):
        high = total.astype(jnp.bfloat16)
        low = (total - high.astype(jnp.float32)).astype(jnp.bfloat16)
        over_rows = (((0,), (0,)), ((), ()))
        product = lax.dot_general(l_ref[s], high, over_rows, preferred_element_type=jnp.float32)
        product += lax.dot_general(l_ref[s], low, over_rows, preferred_element_type=jnp.float32)
        whole, scale = encoded(product)
        term_scale[s] = scale
        for k in range(n_rows):
            term[s, k] = product[k * seg:(k + 1) * seg]
            term_buf[s, k] = whole[k * seg:(k + 1) * seg]

    class both:
        def __init__(self, src, src_scale, dst, dst_scale, send, recv, send_at, recv_at, to_p, to_q):
            self.copies = [
                remote(src, dst, send.at[(0, *send_at)], recv.at[(0, *recv_at)], to_p, to_q),
                remote(src_scale, dst_scale, send.at[(1, *send_at)], recv.at[(1, *recv_at)], to_p, to_q),
            ]

        def start(self):
            for copy in self.copies:
                copy.start()

        def wait_send(self):
            for copy in self.copies:
                copy.wait_send()

        def wait_recv(self):
            for copy in self.copies:
                copy.wait_recv()

    def right_copy(s, d):
        return both(right_buf.at[s, d], right_scale.at[s, d], right_buf.at[s, d], right_scale.at[s, d],
                    r_send, r_recv, (s,), (s, d), p, (q + 1) % n_cols)

    def left_copy(s, d, at):
        last = jnp.where(at == d, n_cols, d)
        return both(left_buf.at[s, d], left_scale.at[s, d], left_buf.at[s, d], left_scale.at[s, d],
                    f_send, r_recv, (s,), (s, last), p, (q + n_cols - 1) % n_cols)

    def right_send(s, d, value):
        right_buf[s, d], right_scale[s, d] = encoded(value)
        right_copy(s, d).start()

    def left_send(s, d, value):
        left_buf[s, d], left_scale[s, d] = encoded(value)
        left_copy(s, d, q - 1).start()

    def line_start(s, nearest):
        @pl.when(q == 0)
        def _():
            for d in ((1,) if nearest else range(n_cols - 1, 1, -1)):
                right_send(s, d, part[s, d])

        @pl.when(q == n_cols - 1)
        def _():
            for d in ((n_cols - 2,) if nearest else range(n_cols - 2)):
                left_send(s, d, part[s, d])

    def relay_right(s, some=slice(None)):
        for d in range(n_cols - 1, 1, -1)[some]:
            @pl.when(jnp.logical_and(q > 0, q < d))
            def _():
                right_copy(s, d).wait_recv()
                right_send(s, d, decoded(right_buf[s, d], right_scale[s, d]) + part[s, d])

    def relay_left(s, some=slice(None)):
        for e in range(n_cols - 2)[some]:
            @pl.when(jnp.logical_and(q < n_cols - 1, q > e))
            def _():
                left_copy(s, e, q).wait_recv()
                left_send(s, e, decoded(left_buf[s, e], left_scale[s, e]) + part[s, e])

    left_half = 2 * q < n_cols - 1

    def relay(s, first, some=slice(None)):
        @pl.when(left_half)
        def _():
            (relay_right if first else relay_left)(s, some)

        @pl.when(jnp.logical_not(left_half))
        def _():
            (relay_left if first else relay_right)(s, some)

    def near(s, source):
        @pl.when(source_chip if source else jnp.logical_not(source_chip))
        def _():
            line_start(s, True)

    def relay_early(s, source, some=slice(None)):
        @pl.when(source_chip if source else jnp.logical_not(source_chip))
        def _():
            relay(s, True, some)

    def line_finish(s):
        @pl.when(q > 0)
        def _():
            right_copy(s, q).wait_recv()
            part[s, q] = part[s, q] + decoded(right_buf[s, q], right_scale[s, q])

        @pl.when(q < n_cols - 1)
        def _():
            left_copy(s, q, q).wait_recv()
            part[s, q] = part[s, q] + decoded(left_buf[s, q], left_scale[s, q])

        y_ref[s] = (-part[s, q]).astype(jnp.bfloat16)
        pltpu.make_async_copy(y_ref.at[s], y_out.at[s], o_sem.at[s, 0]).start()

    def line_drain(s):
        for at in range(n_cols):
            @pl.when(q == at)
            def _():
                for n, buf, scale, send in ((n_cols - 1 - at, right_buf, right_scale, r_send),
                                            (at, left_buf, left_scale, f_send)):
                    if n:
                        some = pl.ds(0, n)
                        both(buf.at[s, some], scale.at[s, some], buf.at[s, some], scale.at[s, some],
                             send, r_recv, (s,), (s, 0), p, (q + 1) % n_cols).wait_send()

    def plane_copy(s, k):
        to = (p + k) % n_rows
        return both(term_buf.at[s, to], term_scale.at[s], plane_buf.at[s, n_rows - k], plane_scale.at[s, n_rows - k],
                    p_send, p_recv, (s,), (s,), to, q)

    def col_copy(s, k):
        to = (q + k) % n_cols
        return both(col_own.at[s], col_own_scale.at[s], col_buf.at[s, q], col_scale.at[s, q],
                    c_send, c_recv, (s,), (s,), p, to)

    def gath_copy(s, k):
        to = (p + k) % n_rows
        return both(own.at[s], own_scale.at[s], g_out.at[s, p], scale_out.at[s, p],
                    g_send, g_recv, (s,), (s,), to, q)

    def all_of(s, n, buf, scale, send, recv):
        some = pl.ds(0, n - 1)
        return both(buf.at[s, some], scale.at[s, some], buf.at[s, some], scale.at[s, some],
                    send, recv, (s,), (s,), pair, q)

    def plane_all(s):
        return all_of(s, n_rows, plane_buf, plane_scale, p_send, p_recv)

    def col_all(s):
        return all_of(s, n_cols, col_buf, col_scale, c_send, c_recv)

    def gath_all(s):
        return all_of(s, n_rows, g_out, scale_out, g_send, g_recv)

    def own_copies(s):
        return [pltpu.make_async_copy(own.at[s], g_out.at[s, p], o_sem.at[s, 1]),
                pltpu.make_async_copy(own_scale.at[s], scale_out.at[s, p], o_sem.at[s, 2])]

    def plane_start(s):
        for k in range(1, n_rows):
            plane_copy(s, k).start()

    def col_start(s):
        total = term[s, p]
        plane_all(s).wait_recv()
        for k in range(1, n_rows):
            total = total + decoded(plane_buf[s, k], plane_scale[s, k])
        col_own[s], col_own_scale[s] = encoded(total)
        for k in range(1, n_cols):
            col_copy(s, k).start()

    def gath_start(s):
        mine_own = decoded(col_own[s], col_own_scale[s])
        col_all(s).wait_recv()
        total = jnp.zeros_like(mine_own)
        for k in range(n_cols):
            total = total + jnp.where(q == k, mine_own, decoded(col_buf[s, k], col_scale[s, k]))
        own[s], own_scale[s] = encoded(total)
        for k in range(1, n_rows):
            gath_copy(s, k).start()
        for copy in own_copies(s):
            copy.start()

    def finish_diagonal(s):
        pltpu.make_async_copy(y_ref.at[s], y_out.at[s], o_sem.at[s, 0]).wait()
        for copy in own_copies(s):
            copy.wait()
        gath_all(s).wait_recv()

    def after(s, total):
        with scope(f"line{s}"):
            line_start(s, False)
            if s + 1 == nodes:
                for i in range(nodes):
                    near(i, True)
        with scope(f"diag{s}"):
            diagonal_term(s, total)
            plane_start(s)

    with scope("frompair"):
        for s in range(nodes):
            for u in range(SUB):
                own_from_pair(s, u)
    def flow(s):
        order = []
        for u in range(SUB):
            order.append((others_from_hi, s, u))
            if s + 1 < nodes:
                order.append((own_from_x, s + 1, u))
        return order

    first = [(own_from_x, 0, u) for u in range(SUB)] + flow(0)
    chosen = 0
    for i, (step, s, u) in enumerate(first):
        ready = STRIPS if i + 1 == len(first) else min(STRIPS, 2 + i * 4 // SUB)
        with scope(f"choose{i}"):
            for k in range(chosen, ready):
                choose(k)
            chosen = ready
        if i + 2 == len(first):
            with scope("own0"):
                multiply_own(0)
        with scope(f"{step.__name__}{s}{u}"):
            step(s, u)
    for s in range(nodes):
        with scope(f"rest{s}"):
            rest(s)
        with scope(f"mult{s}"):
            total = multiply(s)
        after(s, total)
        if s + 1 < nodes:
            order = flow(s + 1)
            for i, (step, to, u) in enumerate(order):
                if 2 * i == len(order):
                    with scope(f"own{s + 1}"):
                        multiply_own(s + 1)
                with scope(f"flow{s + 1}{i}"):
                    step(to, u)
            with scope(f"relayA{s}"):
                relay_early(s, True)
    last = nodes - 1
    for s in range(last):
        with scope(f"relayT{s}"):
            relay_early(s, False)
    for s in range(nodes):
        with scope(f"colstart{s}"):
            col_start(s)
        if s < last:
            with scope(f"relayA{s + 1}"):
                relay_early(s + 1, True)
            with scope(f"relayB{s}"):
                relay(s, False)
    for s in range(nodes):
        near(s, False)
    with scope(f"relayT{last}"):
        relay_early(last, False, slice(0, 1))
    for s in range(last):
        with scope(f"gathstart{s}"):
            gath_start(s)
    with scope(f"relayU{last}"):
        relay_early(last, False, slice(1, None))
    with scope(f"gathstart{last}"):
        gath_start(last)
    with scope(f"relayB{last}"):
        relay(last, False)
    for s in range(nodes):
        with scope(f"finish{s}"):
            line_finish(s)
    with scope("drain"):
        mask_copy.wait()
        for s in range(nodes):
            drain_blocks(s)
            line_drain(s)
            plane_all(s).wait_send()
            col_all(s).wait_send()
    for s in range(nodes):
        with scope(f"findiag{s}"):
            finish_diagonal(s)
    for s in range(nodes):
        with scope("sent"):
            gath_all(s).wait_send()


def put_out(mask_ref, y_ref, whole_ref, scale_ref, d_ref, off_ref, out_ref, off_buf, out_buf, sem):
    nodes, n_rows, seg, _ = whole_ref.shape
    copies = []
    for s in range(nodes):
        value = y_ref[s].astype(jnp.float32)
        for r in range(off_ref.shape[1]):
            off_buf[s, r] = jnp.where(mask_ref[s, r] > 0, value, 0.0).astype(jnp.bfloat16)
        copies.append(pltpu.make_async_copy(off_buf.at[s], off_ref.at[s], sem.at[0, s]))
        copies[-1].start()
        for k in range(n_rows):
            term = whole_ref[s, k].astype(jnp.int32).astype(jnp.float32) * scale_ref[s, k]
            out_buf[s, k * seg:(k + 1) * seg] = d_ref[s, k * seg:(k + 1) * seg] + term
        copies.append(pltpu.make_async_copy(out_buf.at[s], out_ref.at[s], sem.at[1, s]))
        copies[-1].start()
    for copy in copies:
        copy.wait()


def on_device(inverse, panel, structure, diag_inverse):
    n_rows = lax.axis_size("prow")
    n_cols = lax.axis_size("pcol")
    rows_local, block, cols_local, _ = inverse.shape
    nodes, _, _, width = panel.shape
    ratio = n_rows // n_cols
    piece = block // n_cols
    seg = width // n_rows
    strip = block // STRIPS

    vmem = pl.BlockSpec(memory_space=pltpu.VMEM)
    hbm = pl.BlockSpec(memory_space=pltpu.HBM)
    f32, bf16, i16 = jnp.float32, jnp.bfloat16, jnp.int16
    dma = pltpu.SemaphoreType.DMA
    sends = ratio + n_cols // 2 - 1 + ratio
    operands = [pltpu.with_memory_space_constraint(x, pltpu.HBM) for x in (structure, inverse, panel)]
    anywhere = pl.BlockSpec(memory_space=pl.ANY)
    pieces, whole, scale, mask = pl.pallas_call(
        functools.partial(selected, n_rows, n_cols),
        out_shape=(
            jax.ShapeDtypeStruct((nodes, piece, width), bf16),
            jax.ShapeDtypeStruct((nodes, n_rows, seg, width), i16),
            jax.ShapeDtypeStruct((nodes, n_rows, 1, width), f32),
            jax.ShapeDtypeStruct((nodes, rows_local, 1, width), f32),
        ),
        in_specs=[hbm] * 3,
        out_specs=(anywhere,) * 4,
        scratch_shapes=[
            pltpu.SMEM(structure.shape, jnp.int32),
            pltpu.VMEM((nodes, rows_local, 1, width), f32),
            pltpu.VMEM((nodes, piece, width), bf16),
            pltpu.VMEM((nodes, seg, width), i16),
            pltpu.VMEM((nodes, 1, width), f32),
            tuple(pltpu.VMEM(panel.shape[1:], bf16) for _ in range(nodes)),
            tuple(pltpu.VMEM((rows_local, strip, *inverse.shape[2:]), bf16) for _ in range(STRIPS)),
            pltpu.VMEM((nodes, block // 128, strip * cols_local, 128), f32),
            pltpu.VMEM((nodes, ratio, block, block), bf16),
            pltpu.VMEM((nodes, block, width), bf16),
            pltpu.VMEM((nodes, ratio, block, width), bf16),
            pltpu.VMEM((nodes, n_cols, piece, width), f32),
            pltpu.VMEM((nodes, n_cols, piece, width), i16),
            pltpu.VMEM((nodes, n_cols, piece, width), i16),
            pltpu.VMEM((nodes, n_cols, 1, width), f32),
            pltpu.VMEM((nodes, n_cols, 1, width), f32),
            pltpu.VMEM((nodes, n_rows, seg, width), f32),
            pltpu.VMEM((nodes, n_rows, seg, width), i16),
            pltpu.VMEM((nodes, 1, width), f32),
            pltpu.VMEM((nodes, n_rows, seg, width), i16),
            pltpu.VMEM((nodes, n_rows, 1, width), f32),
            pltpu.VMEM((nodes, seg, width), i16),
            pltpu.VMEM((nodes, 1, width), f32),
            pltpu.VMEM((nodes, n_cols, seg, width), i16),
            pltpu.VMEM((nodes, n_cols, 1, width), f32),
            dma, dma, dma((nodes,)), dma((AHEAD,)), dma((nodes, 3)),
            dma((nodes, sends)), dma((nodes, ratio, SUB + 1)),
            dma((2, nodes)), dma((2, nodes)), dma((2, nodes, n_cols + 1)),
            *(dma((2, nodes)) for _ in range(6)),
        ],
        compiler_params=pltpu.CompilerParams(
            collective_id=0, has_side_effects=True, vmem_limit_bytes=50 * 1024 * 1024
        ),
        name="selected_inverse",
    )(*operands)
    return pl.pallas_call(
        put_out,
        out_shape=(
            jax.ShapeDtypeStruct((nodes, rows_local, piece, width), bf16),
            jax.ShapeDtypeStruct(diag_inverse.shape, f32),
        ),
        in_specs=[vmem] * 5,
        out_specs=(hbm, hbm),
        scratch_shapes=[
            pltpu.VMEM((nodes, rows_local, piece, width), bf16),
            pltpu.VMEM(diag_inverse.shape, f32),
            dma((2, nodes)),
        ],
        compiler_params=pltpu.CompilerParams(vmem_limit_bytes=4 * 1024 * 1024),
        name="put_out",
    )(mask, pieces, whole, scale, diag_inverse)


def solution(mesh):
    placed = (P(None, "prow", None, "pcol"), P(None, None, "prow", None), P(), P())
    return jax.shard_map(
        on_device,
        mesh=mesh,
        in_specs=placed,
        out_specs=(P(None, None, ("prow", "pcol"), None), P()),
        check_vma=False,
    )
```

```python
import functools

import jax
import jax.numpy as jnp
from jax import lax
from jax.experimental import pallas as pl
from jax.experimental.pallas import tpu as pltpu
from jax.sharding import PartitionSpec as P

MESH = pl.DeviceIdType.MESH
SUB = 8
STRIPS = 8
AHEAD = 4
FULL = 32700.0


def remote(src, dst, send, recv, p, q):
    return pltpu.make_async_remote_copy(
        src_ref=src, dst_ref=dst, send_sem=send, recv_sem=recv, device_id=(p, q), device_id_type=MESH
    )


def scope(name):
    return jax.named_scope(name)


def find_row(structure_ref, s, residue, n_rows, divisor):
    shift = divisor.bit_length() - 1
    found = jnp.int32(0)
    for i in range(structure_ref.shape[1]):
        value = structure_ref[s, i]
        found = found + jnp.where((value & (n_rows - 1)) == residue, value >> shift, 0)
    return found


def selected(
    n_rows, n_cols, structure_hbm, inverse_ref, panel_ref, y_out, g_out, scale_out, mask_out,
    structure_ref, mask, y_ref, own, own_scale, panel_buf, raw, wide, a_ref, l_ref, l_buf, part,
    right_buf, left_buf, right_scale, left_scale,
    term, term_buf, term_scale, plane_buf, plane_scale, col_own, col_own_scale, col_buf, col_scale,
    s_sem, m_sem, n_sem, a_sem, o_sem,
    l_send, l_recv, r_send, f_send, r_recv, p_send, p_recv, c_send, c_recv, g_send, g_recv,
):
    p = lax.axis_index("prow")
    q = lax.axis_index("pcol")
    nodes, ratio, block, width = l_buf.shape
    rows_local, _, cols_local, _ = inverse_ref.shape
    piece = block // n_cols
    seg = width // n_rows
    chunk = block // (2 * SUB)
    strip = block // STRIPS
    hi = p // n_cols
    lo = p % n_cols
    t = jnp.int32(0)
    bit = 1
    while bit < n_cols:
        t = t + bit * (((lo // bit) + (q // bit)) % 2)
        bit *= 2
    pair = p + 1 - 2 * (p % 2)

    def beside(j):
        lo2 = jnp.int32(0)
        b = 1
        while b < n_cols:
            lo2 = lo2 + b * (((lo // b) + (2 * j // b)) % 2)
            b *= 2
        return hi * n_cols + lo2

    structure_copy = pltpu.make_async_copy(structure_hbm, structure_ref, s_sem)
    structure_copy.start()
    panel_copies = [pltpu.make_async_copy(panel_ref.at[s], panel_buf[s], n_sem.at[s]) for s in range(nodes)]
    for copy in panel_copies:
        copy.start()

    def strip_copy(k):
        part_of = pl.ds(k * strip, strip)
        return pltpu.make_async_copy(inverse_ref.at[:, part_of], raw[k], a_sem.at[k % AHEAD])

    barrier = pltpu.get_barrier_semaphore()
    for k in range(1, n_rows):
        pl.semaphore_signal(barrier, inc=1, device_id=((p + k) % n_rows, q), device_id_type=MESH)
    for k in range(1, n_cols):
        pl.semaphore_signal(barrier, inc=1, device_id=(p, (q + k) % n_cols), device_id_type=MESH)

    def find(s, residue, divisor):
        return find_row(structure_ref, s, residue, n_rows, divisor)

    with scope("pickl"):
        structure_copy.wait()
        row = [find(0, p, n_rows)]
        panel_copies[0].wait()
        l_ref[0] = panel_buf[0][row[0]]
        for k in range(AHEAD):
            strip_copy(k).start()

    with scope("barrier"):
        pl.semaphore_wait(barrier, n_rows + n_cols - 2)

    def rows(c):
        return pl.ds(pl.multiple_of(c * chunk, chunk), chunk)

    def l_slot(s, h, c):
        return l_buf.at[s, h, rows(c)]

    def to_peer_hi(s, c, k, src):
        return remote(src, l_slot(s, hi, c), l_send.at[s, k - 1], l_recv.at[s, hi, c % SUB],
                      (p + k * n_cols) % n_rows, q)

    def to_x(s, c, j, src):
        return remote(src, l_slot(s, hi, c), l_send.at[s, ratio - 1 + j - 1], l_recv.at[s, hi, c % SUB],
                      beside(j), q)

    def to_pair(s, c, k, src):
        h = (hi + k) % ratio
        return remote(src, l_slot(s, h, c), l_send.at[s, ratio - 1 + n_cols // 2 - 1 + k],
                      l_recv.at[s, h, SUB], pair, q)

    def hand_over(s, c):
        return remote(l_ref.at[s, rows(c)], l_slot(s, hi, c), l_send.at[s, 2 * ratio - 1 + n_cols // 2 - 1],
                      l_recv.at[s, hi, c % SUB], pair, q)

    def l_arrived(s, c, h):
        remote(l_slot(s, h, c), l_slot(s, h, c), l_send.at[s, 0], l_recv.at[s, h, c % SUB], pair, q).wait_recv()

    def half(s, h):
        return l_buf.at[s, h, pl.ds(0, SUB * chunk)]

    def half_arrived(s, h):
        remote(half(s, h), half(s, h), l_send.at[s, 0], l_recv.at[s, h, SUB], pair, q).wait_recv()

    def half_sent(s, i):
        remote(half(s, 0), half(s, 0), l_send.at[s, i], l_recv.at[s, 0, 0], pair, q).wait_send()

    owner = t == 0
    source_chip = t < 2
    core = p % 2

    def mine(u):
        return core * SUB + u

    def other(u):
        return (1 - core) * SUB + u

    for s in range(nodes):
        if s > 0:
            row.append(find(s, p, n_rows))
            panel_copies[s].wait()
            l_ref[s] = panel_buf[s][row[s]]

        @pl.when(owner)
        def _():
            for u in range(SUB):
                hand_over(s, other(u)).start()
            for u in range(SUB):
                src = l_ref.at[s, rows(mine(u))]
                for j in range(1, n_cols // 2):
                    to_x(s, mine(u), j, src).start()
                for k in range(1, ratio):
                    to_peer_hi(s, mine(u), k, src).start()
            for u in range(SUB):
                to_pair(s, mine(u), 0, l_ref.at[s, rows(mine(u))]).start()

    cols = [[find(s, h * n_cols + q, n_cols) for h in range(ratio)] for s in range(nodes)]
    for s in range(nodes):
        for r in range(rows_local):
            mask[s, r] = jnp.broadcast_to(jnp.where(row[s] == r, 1.0, 0.0), mask.shape[2:])
    mask_copy = pltpu.make_async_copy(mask, mask_out, m_sem)
    mask_copy.start()

    @pl.when(owner)
    def _():
        for s in range(nodes):
            l_buf[s, hi] = l_ref[s]

    def own_from_pair(s, u):
        c = mine(u)

        @pl.when(t == 1)
        def _():
            l_arrived(s, c, hi)
            for j in range(1, n_cols // 2):
                to_x(s, c, j, l_slot(s, hi, c)).start()
            for k in range(1, ratio):
                to_peer_hi(s, c, k, l_slot(s, hi, c)).start()

    def own_from_x(s, u):
        c = mine(u)

        @pl.when(jnp.logical_not(source_chip))
        def _():
            l_arrived(s, c, hi)
            for k in range(1, ratio):
                to_peer_hi(s, c, k, l_slot(s, hi, c)).start()
            to_pair(s, c, 0, l_slot(s, hi, c)).start()

    def others_from_hi(s, u):
        c = mine(u)
        for k in range(1, ratio):
            l_arrived(s, c, (hi + k) % ratio)
            to_pair(s, c, k, l_slot(s, (hi + k) % ratio, c)).start()

    def rest_own(s):
        @pl.when(jnp.logical_not(owner))
        def _():
            half_arrived(s, hi)

    def rest(s):
        for k in range(1, ratio):
            half_arrived(s, (hi + k) % ratio)

    def drain_blocks(s):
        for k in range(1, ratio):
            half_sent(s, k - 1)
            half_sent(s, ratio - 1 + n_cols // 2 - 1 + k)

        @pl.when(source_chip)
        def _():
            for j in range(1, n_cols // 2):
                half_sent(s, ratio - 1 + j - 1)

        @pl.when(t != 1)
        def _():
            half_sent(s, ratio - 1 + n_cols // 2 - 1)

        @pl.when(owner)
        def _():
            half_sent(s, 2 * ratio - 1 + n_cols // 2 - 1)

    def choose(k):
        strip_copy(k).wait()
        if k + AHEAD < STRIPS:
            strip_copy(k + AHEAD).start()
        for s in range(nodes):
            for b in range(block // 128):
                lanes = raw[k][row[s], :, :, b * 128:(b + 1) * 128].astype(jnp.float32)
                wide[s, b] = lanes.reshape(strip * cols_local, 128)
            for h in range(ratio):
                for b in range(block // 128):
                    a_ref[s, h, k * strip:(k + 1) * strip, b * 128:(b + 1) * 128] = wide[
                        s, b, pl.ds(cols[s][h], strip, stride=cols_local)
                    ].astype(jnp.bfloat16)

    def multiply_own(s):
        rest_own(s)
        total = jnp.dot(a_ref[s, hi], l_buf[s, hi], preferred_element_type=jnp.float32)
        for d in range(n_cols):
            part[s, d] = total[d * piece:(d + 1) * piece]

    def multiply(s):
        h = [(hi + k) % ratio for k in range(1, ratio)]
        total = jnp.dot(a_ref[s, h[0]], l_buf[s, h[0]], preferred_element_type=jnp.float32)
        for k in h[1:]:
            total += jnp.dot(a_ref[s, k], l_buf[s, k], preferred_element_type=jnp.float32)
        total = jnp.concatenate([part[s, d] + total[d * piece:(d + 1) * piece] for d in range(n_cols)], axis=0)
        for d in range(n_cols):
            part[s, d] = total[d * piece:(d + 1) * piece]
        return total

    def encoded(value):
        largest = jnp.maximum(jnp.max(jnp.abs(value), axis=0, keepdims=True), 1e-30)
        whole = jnp.floor(value * (FULL / largest) + 0.5).astype(jnp.int32).astype(jnp.int16)
        return whole, largest * (1.0 / FULL)

    def decoded(whole, scale):
        return whole.astype(jnp.int32).astype(jnp.float32) * scale

    def diagonal_term(s, total):
        high = total.astype(jnp.bfloat16)
        low = (total - high.astype(jnp.float32)).astype(jnp.bfloat16)
        over_rows = (((0,), (0,)), ((), ()))
        product = lax.dot_general(l_ref[s], high, over_rows, preferred_element_type=jnp.float32)
        product += lax.dot_general(l_ref[s], low, over_rows, preferred_element_type=jnp.float32)
        whole, scale = encoded(product)
        term_scale[s] = scale
        for k in range(n_rows):
            term[s, k] = product[k * seg:(k + 1) * seg]
            term_buf[s, k] = whole[k * seg:(k + 1) * seg]

    class both:
        def __init__(self, src, src_scale, dst, dst_scale, send, recv, send_at, recv_at, to_p, to_q):
            self.copies = [
                remote(src, dst, send.at[(0, *send_at)], recv.at[(0, *recv_at)], to_p, to_q),
                remote(src_scale, dst_scale, send.at[(1, *send_at)], recv.at[(1, *recv_at)], to_p, to_q),
            ]

        def start(self):
            for copy in self.copies:
                copy.start()

        def wait_send(self):
            for copy in self.copies:
                copy.wait_send()

        def wait_recv(self):
            for copy in self.copies:
                copy.wait_recv()

    def right_copy(s, d):
        return both(right_buf.at[s, d], right_scale.at[s, d], right_buf.at[s, d], right_scale.at[s, d],
                    r_send, r_recv, (s,), (s, d), p, (q + 1) % n_cols)

    def left_copy(s, d, at):
        last = jnp.where(at == d, n_cols, d)
        return both(left_buf.at[s, d], left_scale.at[s, d], left_buf.at[s, d], left_scale.at[s, d],
                    f_send, r_recv, (s,), (s, last), p, (q + n_cols - 1) % n_cols)

    def right_send(s, d, value):
        right_buf[s, d], right_scale[s, d] = encoded(value)
        right_copy(s, d).start()

    def left_send(s, d, value):
        left_buf[s, d], left_scale[s, d] = encoded(value)
        left_copy(s, d, q - 1).start()

    def line_start(s, nearest):
        @pl.when(q == 0)
        def _():
            for d in ((1,) if nearest else range(n_cols - 1, 1, -1)):
                right_send(s, d, part[s, d])

        @pl.when(q == n_cols - 1)
        def _():
            for d in ((n_cols - 2,) if nearest else range(n_cols - 2)):
                left_send(s, d, part[s, d])

    def relay_right(s, some=slice(None)):
        for d in range(n_cols - 1, 1, -1)[some]:
            @pl.when(jnp.logical_and(q > 0, q < d))
            def _():
                right_copy(s, d).wait_recv()
                right_send(s, d, decoded(right_buf[s, d], right_scale[s, d]) + part[s, d])

    def relay_left(s, some=slice(None)):
        for e in range(n_cols - 2)[some]:
            @pl.when(jnp.logical_and(q < n_cols - 1, q > e))
            def _():
                left_copy(s, e, q).wait_recv()
                left_send(s, e, decoded(left_buf[s, e], left_scale[s, e]) + part[s, e])

    left_half = 2 * q < n_cols - 1

    def relay(s, first, some=slice(None)):
        @pl.when(left_half)
        def _():
            (relay_right if first else relay_left)(s, some)

        @pl.when(jnp.logical_not(left_half))
        def _():
            (relay_left if first else relay_right)(s, some)

    def near(s, source):
        @pl.when(source_chip if source else jnp.logical_not(source_chip))
        def _():
            line_start(s, True)

    def relay_early(s, source, some=slice(None)):
        @pl.when(source_chip if source else jnp.logical_not(source_chip))
        def _():
            relay(s, True, some)

    def line_finish(s):
        @pl.when(q > 0)
        def _():
            right_copy(s, q).wait_recv()
            part[s, q] = part[s, q] + decoded(right_buf[s, q], right_scale[s, q])

        @pl.when(q < n_cols - 1)
        def _():
            left_copy(s, q, q).wait_recv()
            part[s, q] = part[s, q] + decoded(left_buf[s, q], left_scale[s, q])

        y_ref[s] = (-part[s, q]).astype(jnp.bfloat16)
        pltpu.make_async_copy(y_ref.at[s], y_out.at[s], o_sem.at[s, 0]).start()

    def line_drain(s):
        for at in range(n_cols):
            @pl.when(q == at)
            def _():
                for n, buf, scale, send in ((n_cols - 1 - at, right_buf, right_scale, r_send),
                                            (at, left_buf, left_scale, f_send)):
                    if n:
                        some = pl.ds(0, n)
                        both(buf.at[s, some], scale.at[s, some], buf.at[s, some], scale.at[s, some],
                             send, r_recv, (s,), (s, 0), p, (q + 1) % n_cols).wait_send()

    def plane_copy(s, k):
        to = (p + k) % n_rows
        return both(term_buf.at[s, to], term_scale.at[s], plane_buf.at[s, n_rows - k], plane_scale.at[s, n_rows - k],
                    p_send, p_recv, (s,), (s,), to, q)

    def col_copy(s, k):
        to = (q + k) % n_cols
        return both(col_own.at[s], col_own_scale.at[s], col_buf.at[s, q], col_scale.at[s, q],
                    c_send, c_recv, (s,), (s,), p, to)

    def gath_copy(s, k):
        to = (p + k) % n_rows
        return both(own.at[s], own_scale.at[s], g_out.at[s, p], scale_out.at[s, p],
                    g_send, g_recv, (s,), (s,), to, q)

    def all_of(s, n, buf, scale, send, recv):
        some = pl.ds(0, n - 1)
        return both(buf.at[s, some], scale.at[s, some], buf.at[s, some], scale.at[s, some],
                    send, recv, (s,), (s,), pair, q)

    def plane_all(s):
        return all_of(s, n_rows, plane_buf, plane_scale, p_send, p_recv)

    def col_all(s):
        return all_of(s, n_cols, col_buf, col_scale, c_send, c_recv)

    def gath_all(s):
        return all_of(s, n_rows, g_out, scale_out, g_send, g_recv)

    def own_copies(s):
        return [pltpu.make_async_copy(own.at[s], g_out.at[s, p], o_sem.at[s, 1]),
                pltpu.make_async_copy(own_scale.at[s], scale_out.at[s, p], o_sem.at[s, 2])]

    def plane_start(s):
        for k in range(1, n_rows):
            plane_copy(s, k).start()

    def col_start(s):
        total = term[s, p]
        plane_all(s).wait_recv()
        for k in range(1, n_rows):
            total = total + decoded(plane_buf[s, k], plane_scale[s, k])
        col_own[s], col_own_scale[s] = encoded(total)
        for k in range(1, n_cols):
            col_copy(s, k).start()

    def gath_start(s):
        mine_own = decoded(col_own[s], col_own_scale[s])
        col_all(s).wait_recv()
        total = jnp.zeros_like(mine_own)
        for k in range(n_cols):
            total = total + jnp.where(q == k, mine_own, decoded(col_buf[s, k], col_scale[s, k]))
        own[s], own_scale[s] = encoded(total)
        for k in range(1, n_rows):
            gath_copy(s, k).start()
        for copy in own_copies(s):
            copy.start()

    def finish_diagonal(s):
        pltpu.make_async_copy(y_ref.at[s], y_out.at[s], o_sem.at[s, 0]).wait()
        for copy in own_copies(s):
            copy.wait()
        gath_all(s).wait_recv()

    def after(s, total):
        with scope(f"line{s}"):
            line_start(s, False)
            if s + 1 == nodes:
                for i in range(nodes):
                    near(i, True)
        with scope(f"diag{s}"):
            diagonal_term(s, total)
            plane_start(s)

    with scope("frompair"):
        for s in range(nodes):
            for u in range(SUB):
                own_from_pair(s, u)
    def flow(s):
        order = []
        for u in range(SUB):
            order.append((others_from_hi, s, u))
            if s + 1 < nodes:
                order.append((own_from_x, s + 1, u))
        return order

    first = [(own_from_x, 0, u) for u in range(SUB)] + flow(0)
    chosen = 0
    for i, (step, s, u) in enumerate(first):
        ready = STRIPS if i + 1 == len(first) else min(STRIPS, 2 + i * 4 // SUB)
        with scope(f"choose{i}"):
            for k in range(chosen, ready):
                choose(k)
            chosen = ready
        if i + 2 == len(first):
            with scope("own0"):
                multiply_own(0)
        with scope(f"{step.__name__}{s}{u}"):
            step(s, u)
    for s in range(nodes):
        with scope(f"rest{s}"):
            rest(s)
        with scope(f"mult{s}"):
            total = multiply(s)
        after(s, total)
        if s + 1 < nodes:
            order = flow(s + 1)
            for i, (step, to, u) in enumerate(order):
                if 2 * i == len(order):
                    with scope(f"own{s + 1}"):
                        multiply_own(s + 1)
                with scope(f"flow{s + 1}{i}"):
                    step(to, u)
            with scope(f"relayA{s}"):
                relay_early(s, True)
    last = nodes - 1
    for s in range(last):
        with scope(f"relayT{s}"):
            relay_early(s, False)
    for s in range(nodes):
        with scope(f"colstart{s}"):
            col_start(s)
        if s < last:
            with scope(f"relayA{s + 1}"):
                relay_early(s + 1, True)
            with scope(f"relayB{s}"):
                relay(s, False)
    for s in range(nodes):
        near(s, False)
    with scope(f"relayT{last}"):
        relay_early(last, False, slice(0, 1))
    for s in range(last):
        with scope(f"gathstart{s}"):
            gath_start(s)
    with scope(f"gathstart{last}"):
        gath_start(last)
    with scope(f"relayU{last}"):
        relay_early(last, False, slice(1, None))
    with scope(f"relayB{last}"):
        relay(last, False)
    for s in range(nodes):
        with scope(f"finish{s}"):
            line_finish(s)
    with scope("drain"):
        mask_copy.wait()
        for s in range(nodes):
            drain_blocks(s)
            line_drain(s)
            plane_all(s).wait_send()
            col_all(s).wait_send()
    for s in range(nodes):
        with scope(f"findiag{s}"):
            finish_diagonal(s)
    for s in range(nodes):
        with scope("sent"):
            gath_all(s).wait_send()


def put_out(mask_ref, y_ref, whole_ref, scale_ref, d_ref, off_ref, out_ref, off_buf, out_buf, sem):
    nodes, n_rows, seg, _ = whole_ref.shape
    copies = []
    for s in range(nodes):
        value = y_ref[s].astype(jnp.float32)
        for r in range(off_ref.shape[1]):
            off_buf[s, r] = jnp.where(mask_ref[s, r] > 0, value, 0.0).astype(jnp.bfloat16)
        copies.append(pltpu.make_async_copy(off_buf.at[s], off_ref.at[s], sem.at[0, s]))
        copies[-1].start()
        for k in range(n_rows):
            term = whole_ref[s, k].astype(jnp.int32).astype(jnp.float32) * scale_ref[s, k]
            out_buf[s, k * seg:(k + 1) * seg] = d_ref[s, k * seg:(k + 1) * seg] + term
        copies.append(pltpu.make_async_copy(out_buf.at[s], out_ref.at[s], sem.at[1, s]))
        copies[-1].start()
    for copy in copies:
        copy.wait()


def on_device(inverse, panel, structure, diag_inverse):
    n_rows = lax.axis_size("prow")
    n_cols = lax.axis_size("pcol")
    rows_local, block, cols_local, _ = inverse.shape
    nodes, _, _, width = panel.shape
    ratio = n_rows // n_cols
    piece = block // n_cols
    seg = width // n_rows
    strip = block // STRIPS

    vmem = pl.BlockSpec(memory_space=pltpu.VMEM)
    hbm = pl.BlockSpec(memory_space=pltpu.HBM)
    f32, bf16, i16 = jnp.float32, jnp.bfloat16, jnp.int16
    dma = pltpu.SemaphoreType.DMA
    sends = ratio + n_cols // 2 - 1 + ratio
    operands = [pltpu.with_memory_space_constraint(x, pltpu.HBM) for x in (structure, inverse, panel)]
    anywhere = pl.BlockSpec(memory_space=pl.ANY)
    pieces, whole, scale, mask = pl.pallas_call(
        functools.partial(selected, n_rows, n_cols),
        out_shape=(
            jax.ShapeDtypeStruct((nodes, piece, width), bf16),
            jax.ShapeDtypeStruct((nodes, n_rows, seg, width), i16),
            jax.ShapeDtypeStruct((nodes, n_rows, 1, width), f32),
            jax.ShapeDtypeStruct((nodes, rows_local, 1, width), f32),
        ),
        in_specs=[hbm] * 3,
        out_specs=(anywhere,) * 4,
        scratch_shapes=[
            pltpu.SMEM(structure.shape, jnp.int32),
            pltpu.VMEM((nodes, rows_local, 1, width), f32),
            pltpu.VMEM((nodes, piece, width), bf16),
            pltpu.VMEM((nodes, seg, width), i16),
            pltpu.VMEM((nodes, 1, width), f32),
            tuple(pltpu.VMEM(panel.shape[1:], bf16) for _ in range(nodes)),
            tuple(pltpu.VMEM((rows_local, strip, *inverse.shape[2:]), bf16) for _ in range(STRIPS)),
            pltpu.VMEM((nodes, block // 128, strip * cols_local, 128), f32),
            pltpu.VMEM((nodes, ratio, block, block), bf16),
            pltpu.VMEM((nodes, block, width), bf16),
            pltpu.VMEM((nodes, ratio, block, width), bf16),
            pltpu.VMEM((nodes, n_cols, piece, width), f32),
            pltpu.VMEM((nodes, n_cols, piece, width), i16),
            pltpu.VMEM((nodes, n_cols, piece, width), i16),
            pltpu.VMEM((nodes, n_cols, 1, width), f32),
            pltpu.VMEM((nodes, n_cols, 1, width), f32),
            pltpu.VMEM((nodes, n_rows, seg, width), f32),
            pltpu.VMEM((nodes, n_rows, seg, width), i16),
            pltpu.VMEM((nodes, 1, width), f32),
            pltpu.VMEM((nodes, n_rows, seg, width), i16),
            pltpu.VMEM((nodes, n_rows, 1, width), f32),
            pltpu.VMEM((nodes, seg, width), i16),
            pltpu.VMEM((nodes, 1, width), f32),
            pltpu.VMEM((nodes, n_cols, seg, width), i16),
            pltpu.VMEM((nodes, n_cols, 1, width), f32),
            dma, dma, dma((nodes,)), dma((AHEAD,)), dma((nodes, 3)),
            dma((nodes, sends)), dma((nodes, ratio, SUB + 1)),
            dma((2, nodes)), dma((2, nodes)), dma((2, nodes, n_cols + 1)),
            *(dma((2, nodes)) for _ in range(6)),
        ],
        compiler_params=pltpu.CompilerParams(
            collective_id=0, has_side_effects=True, vmem_limit_bytes=50 * 1024 * 1024
        ),
        name="selected_inverse",
    )(*operands)
    return pl.pallas_call(
        put_out,
        out_shape=(
            jax.ShapeDtypeStruct((nodes, rows_local, piece, width), bf16),
            jax.ShapeDtypeStruct(diag_inverse.shape, f32),
        ),
        in_specs=[vmem] * 5,
        out_specs=(hbm, hbm),
        scratch_shapes=[
            pltpu.VMEM((nodes, rows_local, piece, width), bf16),
            pltpu.VMEM(diag_inverse.shape, f32),
            dma((2, nodes)),
        ],
        compiler_params=pltpu.CompilerParams(vmem_limit_bytes=4 * 1024 * 1024),
        name="put_out",
    )(mask, pieces, whole, scale, diag_inverse)


def solution(mesh):
    placed = (P(None, "prow", None, "pcol"), P(None, None, "prow", None), P(), P())
    return jax.shard_map(
        on_device,
        mesh=mesh,
        in_specs=placed,
        out_specs=(P(None, None, ("prow", "pcol"), None), P()),
        check_vma=False,
    )
```
